256 devices in a mesh: dp: 2 (over core), seq: 128 (over z, y, x).
Axes of the slice: x: 4, y: 4, z: 8, core: 2. Of those that a mesh axis runs over, the one named last changes fastest.
Arguments:
- joints_x: bfloat16 [2, 256, 128, 1536], P('dp', 'seq'), may hold values from -6 to 6
- cotangent: bfloat16 [2, 256, 128, 1536], P('dp', 'seq'), may hold values from -6 to 6
- hidden: int32 [2, 256, 128], P('dp', 'seq'), may hold values 0 or 1
- stream_clip: int32 [2, 256], P('dp'), may hold values from 0 to 271, as said below
- stream_kind: int32 [2, 256], P('dp'), may hold values from 0 to 3, as said below
- adjacency: int32 [4, 136, 136], replicated, may hold values 0 or 1
- mask_token: bfloat16 [1536], replicated, may hold values from -6 to 6
- norm_gain: float32 [1536], replicated, may hold values from 0.1 to 1.9
- w_qkv: bfloat16 [1536, 2304], replicated, may hold values from -0.15625 to 0.15625
- w_out: bfloat16 [768, 1536], replicated, may hold values from -0.21875 to 0.21875
- graph_coef: float32 [12], replicated, may hold values from 0.5 to 260
Outputs:
- layer_out: bfloat16 [2, 256, 128, 1536], P('dp', 'seq')
- grad_x: bfloat16 [2, 256, 128, 1536], P('dp', 'seq')
- grad_token: float32 [1536], replicated
- grad_gain: float32 [1536], replicated
- grad_coef: float32 [12], replicated
The draws below stay inside these ranges and needn't reach their ends.
Inputs may be any that keep to these rules, and one draw needn't show every extreme that they name: `stream_clip`: the slots of a clip are consecutive, clip numbers rise in slot order, starting at 0, at most 16 of them; every slot after the last clip, the last slot always among them, is padding numbered 16 plus its slot index. `stream_kind`: constant within a clip; a clip of kind 0, 1, 2, 3 has 17, 25, 52, 133 slots; slot 0 starts a clip of kind 3; padding slots have kind 0.
All inputs are finite; a program needn't handle non-finite values. No bound on the sum of `hidden` on one device may be relied on, other than what follows from the above.
Results may differ from the reference program's by a relative error of at most 0.0089.
Values may be sent and summed in bfloat16 or wider, within the bound.
A program may use at most 128 MiB of HBM per device.

```python
import jax
import jax.numpy as jnp
from jax import lax

D = 1536
HEADS = 12
HW = 768
JS = 256
L = 128
NB = 2
KINDS = 4
JMAX = 136


def stream_tables(key):

    def per_batch(batch_idx):
        batch_key = jax.random.fold_in(jax.random.fold_in(key, 101), batch_idx)
        kind_draw = jax.random.randint(batch_key, (16,), 0, 4).astype(jnp.int32).at[0].set(3)
        clip_sizes = jnp.array([17, 25, 52, 133], jnp.int32)[kind_draw]

        def pack_step(position, clip_size):
            clip_fits = position + clip_size <= JS - 1
            clip_start = jnp.where(clip_fits, position, JS)
            clip_stop = jnp.where(clip_fits, position + clip_size, JS)
            return (jnp.where(clip_fits, position + clip_size, position), (clip_start, clip_stop))
        _, (starts, stops) = lax.scan(pack_step, jnp.int32(0), clip_sizes)
        slot_ids = jnp.arange(JS, dtype=jnp.int32)
        in_clip = (slot_ids[:, None] >= starts[None, :]) & (slot_ids[:, None] < stops[None, :])
        is_placed = jnp.any(in_clip, axis=1)
        numbers = jnp.arange(16, dtype=jnp.int32)
        clip_ids = jnp.where(is_placed, jnp.sum(in_clip.astype(jnp.int32) * numbers[None, :], axis=1), 16 + slot_ids)
        kind_ids = jnp.where(is_placed, jnp.sum(in_clip.astype(jnp.int32) * kind_draw[None, :], axis=1), 0)
        return (clip_ids.astype(jnp.int32), kind_ids.astype(jnp.int32))
    return jax.vmap(per_batch)(jnp.arange(NB, dtype=jnp.int32))


def draw_stream_clip(key, part):
    return stream_tables(key)[0]


def draw_stream_kind(key, part):
    return stream_tables(key)[1]


def draw_graph_coef(key, part):
    base_values = jax.random.uniform(jax.random.fold_in(key, 3), (HEADS,), jnp.float32, 0.5, 3.0)
    return base_values


def set_ends(entries, key, smallest, top_value):
    shape = entries.shape
    place = [jax.random.randint(jax.random.fold_in(key, axis), (), 0, shape[axis]) for axis in range(len(shape))]
    entries = entries.at[tuple(place)].set(smallest)
    longest = shape.index(max(shape))
    place[longest] = (place[longest] + 1) % shape[longest]
    return entries.at[tuple(place)].set(top_value)


def shard_levels(key, shape, split, smallest, top_value):
    factor_of = 1.0
    for dim, blocks in split:
        steps = jax.random.uniform(jax.random.fold_in(jax.random.fold_in(key, 6), dim), (blocks,), jnp.float32, smallest / len(split), top_value / len(split))
        factor_of = factor_of * jnp.repeat(jnp.exp(steps), shape[dim] // blocks).reshape((-1,) + (1,) * (len(shape) - 1 - dim))
    return factor_of


def scatter_about(rng, dims, deviation, most, pieces=(), kind=jnp.bfloat16):
    result = deviation * jax.random.normal(rng, dims, jnp.float32)
    if pieces:
        result = result * shard_levels(rng, dims, pieces, -0.22, 0.18)
    return jnp.clip(result, -most, most).astype(kind)


def setup_inputs(seed: int = 0) -> dict:
    keys = jax.random.split(jax.random.key(seed), 12)
    return {
        "joints_x": scatter_about(keys[0], (NB, JS, L, D), 1.0, 6.0, ((0, 2), (1, 128))),
        "cotangent": scatter_about(keys[1], (NB, JS, L, D), 1.0, 6.0, ((0, 2), (1, 128))),
        "hidden": set_ends((jax.random.randint(keys[2], (NB, JS, L), 0, 10) < 3).astype(jnp.int32), jax.random.fold_in(keys[2], 1), 0, 1),
        "stream_clip": draw_stream_clip(jax.random.fold_in(keys[11], 71), 0),
        "stream_kind": draw_stream_kind(jax.random.fold_in(keys[11], 71), 0),
        "adjacency": set_ends((jax.random.randint(keys[5], (KINDS, JMAX, JMAX), 0, 6) < 1).astype(jnp.int32), jax.random.fold_in(keys[5], 1), 0, 1),
        "mask_token": scatter_about(keys[6], (D,), 1.0, 6.0),
        "norm_gain": jnp.clip(1.0 + 0.18 * jax.random.normal(keys[7], (D,), jnp.float32), 0.1, 1.9),
        "w_qkv": scatter_about(keys[8], (D, 3 * HW), D ** -0.5, 0.15625),
        "w_out": scatter_about(keys[9], (HW, D), HW ** -0.5, 0.21875),
        "graph_coef": draw_graph_coef(jax.random.fold_in(keys[11], 71), 0),
    }


def product(form, left, right):
    return jnp.einsum(form, left.astype(jnp.float32), right.astype(jnp.float32))

def frame_tables(clip_ids, kind_ids, adjacency):
    slot_count = clip_ids.shape[0]
    kind_count, joint_max = (adjacency.shape[0], adjacency.shape[1])
    slot_ids = jnp.arange(slot_count, dtype=jnp.int32)
    same_clip = clip_ids[:, None] == clip_ids[None, :]
    first_slot = lax.optimization_barrier(jnp.min(jnp.where(same_clip, slot_ids[None, :], slot_count), axis=1)).astype(jnp.int32)
    joint_idx = slot_ids - first_slot
    table_row = kind_ids * joint_max + joint_idx
    row_pick = (table_row[:, None] == jnp.arange(kind_count * joint_max, dtype=jnp.int32)[None, :]).astype(jnp.float32)
    adj_table = adjacency.reshape(kind_count * joint_max, joint_max).astype(jnp.float32)
    picked = jnp.dot(row_pick, adj_table, precision=lax.Precision.HIGHEST, preferred_element_type=jnp.float32)
    col_pick = (joint_idx[:, None] == jnp.arange(joint_max, dtype=jnp.int32)[None, :]).astype(jnp.float32)
    graph_link = jnp.dot(picked, col_pick.T, precision=lax.Precision.HIGHEST, preferred_element_type=jnp.float32)
    return (same_clip, graph_link)

def attend(x_normed, same_clip, graph_link, graph_coef, w_qkv, w_out):
    slot_count, frame_count = (x_normed.shape[0], x_normed.shape[1])
    head_count = graph_coef.shape[0]
    head_width = w_out.shape[0]
    head_size = head_width // head_count
    score_scale = head_size ** (-0.5)
    united = product('jfd,de->jfe', x_normed, w_qkv).astype(jnp.bfloat16)
    query_part = united[..., :head_width].reshape(slot_count, frame_count, head_count, head_size)
    key_part = united[..., head_width:2 * head_width].reshape(slot_count, frame_count, head_count, head_size)
    value_part = united[..., 2 * head_width:].reshape(slot_count, frame_count, head_count, head_size)
    scores = product('ifhc,jfhc->fhij', query_part, key_part) * score_scale
    scores = scores + graph_coef[None, :, None, None] * graph_link[None, None]
    scores = jnp.where(same_clip[None, None], scores, -jnp.inf)
    row_top = lax.optimization_barrier(jnp.max(scores, axis=-1, keepdims=True))
    shifted = jnp.exp(scores - row_top)
    weights_f = shifted / lax.optimization_barrier(jnp.sum(shifted, axis=-1, keepdims=True))
    weights_b = weights_f.astype(jnp.bfloat16)
    context = product('fhij,jfhc->ifhc', weights_b, value_part).astype(jnp.bfloat16)
    context = context.reshape(slot_count, frame_count, head_width)
    attn_out = product('jfe,ed->jfd', context, w_out).astype(jnp.bfloat16)
    return (attn_out, (query_part, key_part, value_part, weights_f, weights_b))

def attend_back(cot_rows, saved, graph_link, w_qkv, w_out):
    query_part, key_part, value_part, weights_f, weights_b = saved
    slot_count, frame_count, head_count, head_size = query_part.shape
    head_width = head_count * head_size
    score_scale = head_size ** (-0.5)
    grad_context = product('jfd,ed->jfe', cot_rows, w_out).astype(jnp.bfloat16)
    grad_context = grad_context.reshape(slot_count, frame_count, head_count, head_size)
    grad_weights = product('ifhc,jfhc->fhij', grad_context, value_part)
    row_total = lax.optimization_barrier(jnp.sum(weights_f * grad_weights, axis=-1, keepdims=True))
    grad_scores = weights_f * (grad_weights - row_total)
    coef_term = lax.optimization_barrier(jnp.sum(grad_scores * graph_link[None, None], axis=(0, 2, 3)))
    scaled_b = (grad_scores * score_scale).astype(jnp.bfloat16)
    grad_query = product('fhij,jfhc->ifhc', scaled_b, key_part).reshape(slot_count, frame_count, head_width)
    grad_key = product('fhij,ifhc->jfhc', scaled_b, query_part).reshape(slot_count, frame_count, head_width)
    grad_value = product('fhij,ifhc->jfhc', weights_b, grad_context).reshape(slot_count, frame_count, head_width)
    grad_united = jnp.concatenate([grad_query, grad_key, grad_value], axis=-1).astype(jnp.bfloat16)
    grad_normed = product('jfe,de->jfd', grad_united, w_qkv).astype(jnp.bfloat16)
    return (grad_normed, coef_term)

def normalize(x_rows, hidden_on, mask_token, norm_gain):
    x_in = jnp.where(hidden_on, mask_token, x_rows)
    x_float = x_in.astype(jnp.float32)
    root_mean = jnp.sqrt(lax.optimization_barrier(jnp.mean(x_float * x_float, axis=-1, keepdims=True)) + 1e-06)
    x_unit = x_float / root_mean
    x_normed = (x_unit * norm_gain).astype(jnp.bfloat16)
    return (x_float, root_mean, x_unit, x_normed)

def finish(x_float, root_mean, x_unit, hidden_on, attn_back, grad_normed, cot_rows, norm_gain):
    layer_out = (x_float + attn_back.astype(jnp.float32)).astype(jnp.bfloat16)
    gain_grad = grad_normed.astype(jnp.float32) * norm_gain
    grad_input = cot_rows.astype(jnp.float32) + (gain_grad - x_unit * lax.optimization_barrier(jnp.mean(gain_grad * x_unit, axis=-1, keepdims=True))) / root_mean
    grad_x = jnp.where(hidden_on, jnp.float32(0.0), grad_input).astype(jnp.bfloat16)
    lead_axes = tuple(range(grad_input.ndim - 1))
    token_term = lax.optimization_barrier(jnp.sum(jnp.where(hidden_on, grad_input, jnp.float32(0.0)), axis=lead_axes))
    gain_term = lax.optimization_barrier(jnp.sum(grad_normed.astype(jnp.float32) * x_unit, axis=lead_axes))
    return (layer_out, grad_x, token_term, gain_term)

def reference(joints_x, cotangent, hidden, stream_clip, stream_kind, adjacency, mask_token, norm_gain, w_qkv, w_out, graph_coef):
    hidden_on = (hidden == 1)[..., None]
    x_float, root_mean, x_unit, x_normed = normalize(joints_x, hidden_on, mask_token, norm_gain)
    attn_parts = []
    grad_parts = []
    coef_total = jnp.zeros((graph_coef.shape[0],), jnp.float32)
    for batch_idx in range(joints_x.shape[0]):
        same_clip, graph_link = frame_tables(stream_clip[batch_idx], stream_kind[batch_idx], adjacency)
        frames_x = jnp.swapaxes(x_normed[batch_idx], 0, 1)[:, :, None, :]
        frames_cot = jnp.swapaxes(cotangent[batch_idx], 0, 1)[:, :, None, :]

        def per_frame(pair_item, same_clip=same_clip, graph_link=graph_link):
            attn_out, saved = attend(pair_item[0], same_clip, graph_link, graph_coef, w_qkv, w_out)
            grad_normed, coef_term = attend_back(pair_item[1], saved, graph_link, w_qkv, w_out)
            return (attn_out, grad_normed, coef_term)
        outs_attn, outs_grad, coef_terms = lax.map(per_frame, (frames_x, frames_cot))
        attn_parts.append(jnp.swapaxes(outs_attn[:, :, 0, :], 0, 1))
        grad_parts.append(jnp.swapaxes(outs_grad[:, :, 0, :], 0, 1))
        coef_total = coef_total + lax.optimization_barrier(jnp.sum(coef_terms, axis=0))
    attn_back = jnp.stack(attn_parts)
    grad_normed = jnp.stack(grad_parts)
    layer_out, grad_x, token_term, gain_term = finish(x_float, root_mean, x_unit, hidden_on, attn_back, grad_normed, cotangent, norm_gain)
    return (layer_out, grad_x, token_term, gain_term, coef_total)
```

```python
import functools

import jax
import jax.numpy as jnp
from jax import lax
from jax.experimental import pallas as pl
from jax.experimental.pallas import tpu as pltpu
from jax.sharding import PartitionSpec as P

MESH = pl.DeviceIdType.MESH
BF = jnp.bfloat16
F32 = jnp.float32
NSEQ = 128
XY = 16
NZ = 8
D = 1536
HW = 768
HEADS = 12
HD = 64
R = 256
L = 128
KINDS = 4
JM = 136
PAIRS = HEADS // 2


def iota(shape, axis):
    return lax.broadcasted_iota(jnp.int32, shape, axis)


def nn(a, b):
    return jnp.dot(a, b, preferred_element_type=F32)


def nt(a, b):
    return lax.dot_general(a, b, (((1,), (1,)), ((), ())), preferred_element_type=F32)


def to_column(row, n):
    diag = iota((n, n), 0) == iota((n, n), 1)
    return jnp.sum(jnp.where(diag, row, jnp.zeros_like(row)), axis=1, keepdims=True)


def fused_kernel(
    x_hbm,
    cot_hbm,
    hid_hbm,
    clip_hbm,
    kind_hbm,
    adj_hbm,
    tok_hbm,
    gain_hbm,
    wqkv_hbm,
    wout_hbm,
    coef_ref,
    out_hbm,
    gx_hbm,
    token_ref,
    gain_out_ref,
    coef_out_ref,
    xv,
    cotv,
    hidv,
    clipv,
    kindv,
    adjv,
    tokv,
    gainv,
    wq,
    wo,
    outv,
    gxv,
    xs,
    xr,
    gs,
    gr,
    cs,
    cr,
    ns,
    nr,
    hcol,
    rcol,
    qkv,
    xn,
    gc,
    vt,
    kt,
    ctt,
    pts,
    du,
    link,
    neg,
    coefs,
    tmp,
    a0,
    b1,
    b2,
    b3,
    in_sem,
    send_sem,
    recv_sem,
    loc_sem,
    out_sem,
):
    me = lax.axis_index("seq")
    core = lax.axis_index("dp")
    z = me // XY
    yx = me % XY
    y = yx // 4
    x = yx % 4

    loads = [
        (x_hbm.at[0], xv),
        (hid_hbm, hidv),
        (tok_hbm, tokv),
        (gain_hbm, gainv),
        (cot_hbm.at[0], cotv),
        (wout_hbm, wo),
        (clip_hbm, clipv),
        (kind_hbm, kindv),
        (adj_hbm, adjv),
        (wqkv_hbm, wq),
    ]
    load = [pltpu.make_async_copy(s, d, in_sem.at[i]) for i, (s, d) in enumerate(loads)]
    for c in load:
        c.start()

    barrier = pltpu.get_barrier_semaphore()

    def greet(k, _):
        pl.semaphore_signal(
            barrier, inc=1, device_id={"seq": (me + k) % NSEQ}, device_id_type=MESH
        )
        return 0

    lax.fori_loop(1, NSEQ, greet, 0)

    def greet_other(k, _):
        pl.semaphore_signal(
            barrier,
            inc=1,
            device_id={"dp": 1 - core, "seq": k * XY + yx},
            device_id_type=MESH,
        )
        return 0

    lax.fori_loop(0, NZ, greet_other, 0)

    for c in load[:4]:
        c.wait()
    tok = tokv[...].astype(F32)
    gain = gainv[...]
    hid = hidv[0].astype(F32)
    for s in range(2):
        hcol[s] = to_column(hid[s : s + 1, :], L)
    pl.semaphore_wait(barrier, NSEQ - 1 + NZ)

    def peer(dz, dyx):
        return ((z + dz) % NZ) * XY + ((y + dyx // 4) % 4) * 4 + (x + dyx % 4) % 4

    def send(src, dst, phase, to):
        return pltpu.make_async_remote_copy(
            src_ref=src,
            dst_ref=dst,
            send_sem=send_sem.at[phase],
            recv_sem=recv_sem.at[phase],
            device_id={"seq": to},
            device_id_type=MESH,
        )

    def send_all(src, dst, phase):
        pltpu.make_async_copy(src.at[me], dst.at[me], loc_sem.at[phase]).start()

        def body(k, _):
            to = peer(k % NZ, k // NZ)
            send(src.at[to], dst.at[me], phase, to).start()
            return 0

        lax.fori_loop(1, NSEQ, body, 0)

    def drain(ref, sem):
        part = ref.at[pl.ds(0, NSEQ - 1)]
        pltpu.make_async_copy(part, part, sem).wait()

    def arrived(src, dst, phase):
        pltpu.make_async_copy(src.at[me], dst.at[me], loc_sem.at[phase]).wait()
        drain(dst, recv_sem.at[phase])

    r32, c32 = iota((32, 32), 0), iota((32, 32), 1)
    mix32 = (c32 == (r32 % 2) * 16 + r32 // 2).astype(BF)

    def norm_step(i, _):
        dz = jnp.where(i == NZ - 1, 0, (i // 2) + 1)
        dz = jnp.where(i % 2 == 1, jnp.where(i == NZ - 1, 0, NZ - dz), dz)
        zz = (z + dz) % NZ
        f0 = pl.multiple_of(zz * XY, XY)
        parts = []
        for s in range(2):
            xf = xv[s, pl.ds(f0, XY), :].astype(F32)
            h = hcol[s, pl.ds(f0, XY), :]
            xf = jnp.where(h > 0.5, tok, xf)
            rinv = 1.0 / jnp.sqrt(jnp.mean(xf * xf, axis=1, keepdims=True) + 1e-06)
            rcol[s, pl.ds(f0, XY), :] = rinv
            parts.append((xf * rinv * gain).astype(BF))
        both = nn(mix32, jnp.concatenate(parts, axis=0)).astype(BF)
        xs[pl.ds(f0, XY)] = both.reshape(XY, 2, D)

        def body(k, _):
            to = zz * XY + ((y + k // 4) % 4) * 4 + (x + k % 4) % 4

            @pl.when(to != me)
            def _():
                send(xs.at[to], xr.at[me], 0, to).start()

            return 0

        lax.fori_loop(0, XY, body, 0)
        return 0

    lax.fori_loop(0, NZ, norm_step, 0)
    pltpu.make_async_copy(xs.at[me], xr.at[me], loc_sem.at[0]).start()

    ri, ci = iota((R, R), 0), iota((R, R), 1)
    mix = (ci == (ri % 2) * L + ri // 2).astype(BF)
    unmix = (ci == (ri % L) * 2 + ri // L).astype(BF)
    for c in load[4:6]:
        c.wait()

    @pl.loop(0, HW // 256)
    def _(n):
        n0 = pl.multiple_of(n * 256, 256)
        part = nt(cotv[...].reshape(R, D), wo[pl.ds(n0, 256), :]).astype(BF)
        tmp[:, pl.ds(n0, 256)] = nn(mix, part).astype(BF)

    gs[...] = tmp[:, :HW].reshape(NSEQ, 2, HW)
    send_all(gs, gr, 1)

    for c in load[6:9]:
        c.wait()
    clip_row = clipv[...]
    clip_col = to_column(clip_row, R)
    same = clip_col == clip_row
    first_row = jnp.min(jnp.where(same, ri, R), axis=0, keepdims=True)
    first_col = to_column(first_row, R)
    kind_col = to_column(kindv[...], R)
    joint_col = iota((R, 1), 0) - first_col
    pick = iota((R, JM), 1) == joint_col
    picked = jnp.zeros((R, JM), F32)
    for k in range(KINDS):
        rows = (pick & (kind_col == k)).astype(BF)
        picked = picked + nn(rows, adjv[k].astype(F32).astype(BF))
    link[...] = nt(pick.astype(BF), picked.astype(BF))
    neg[...] = jnp.where(same, jnp.float32(0.0), -jnp.inf)

    load[9].wait()
    arrived(xs, xr, 0)
    xn[...] = xr[...].reshape(R, D)

    @pl.loop(0, 3 * HW // 256)
    def _(n):
        n0 = pl.multiple_of(n * 256, 256)
        part = nn(xn[...], wq[:, pl.ds(n0, 256)]).astype(BF)
        scale = jnp.where(n < HW // 256, HD**-0.5, 1.0).astype(BF)
        qkv[:, pl.ds(n0, 256)] = part * scale

    coefs[...] = jnp.zeros_like(coefs)
    kt[...] = qkv[:, HW : 2 * HW].T
    vt[...] = qkv[:, 2 * HW :].T

    lane = iota((R, 128), 1)

    @pl.loop(0, PAIRS)
    def _(j):
        c0 = pl.multiple_of(j * 128, 128)
        q2 = qkv[:, pl.ds(c0, 128)]
        k2 = qkv[:, pl.ds(HW + c0, 128)]
        for i in range(2):
            h = j * 2 + i
            kh = jnp.where((lane < HD) == (i == 0), k2, jnp.zeros_like(k2))
            st = nt(kh, q2) + (coef_ref[h] * link[...] + neg[...])
            e = jnp.exp(st - jnp.max(st, axis=0, keepdims=True))
            pt = e * (1.0 / jnp.sum(e, axis=0, keepdims=True))
            pts[h] = pt
            r0 = pl.multiple_of(h * HD, HD)
            ctt[pl.ds(r0, HD), :] = nn(vt[pl.ds(r0, HD), :], pt.astype(BF)).astype(BF)

    cs[...] = ctt[...].T.reshape(NSEQ, 2, HW)
    send_all(cs, cr, 2)

    arrived(gs, gr, 1)
    gc[...] = gr[...].reshape(R, HW)

    @pl.loop(0, PAIRS)
    def _(j):
        c0 = pl.multiple_of(j * 128, 128)
        q2 = qkv[:, pl.ds(c0, 128)]
        v2 = qkv[:, pl.ds(2 * HW + c0, 128)]
        g2 = gc[:, pl.ds(c0, 128)]
        dk, dv = [], []
        for i in range(2):
            h = j * 2 + i
            vh = jnp.where((lane < HD) == (i == 0), v2, jnp.zeros_like(v2))
            dp = nt(vh, g2)
            pt = pts[h]
            ds = pt * (dp - jnp.sum(pt * dp, axis=0, keepdims=True))
            coefs[pl.ds(h, 1), :] = jnp.sum(ds * link[...], axis=0, keepdims=True)
            db = ds.astype(BF)
            r0 = pl.multiple_of(h * HD, HD)
            dq = nn(kt[pl.ds(r0, HD), :], db) * (HD**-0.5)
            ctt[pl.ds(r0, HD), :] = dq.astype(BF)
            dk.append(nn(db, q2))
            dv.append(nn(pt.astype(BF), g2))
        du[:, pl.ds(HW + c0, 128)] = jnp.where(lane < HD, dk[0], dk[1]).astype(BF)
        du[:, pl.ds(2 * HW + c0, 128)] = jnp.where(lane < HD, dv[0], dv[1]).astype(BF)

    du[:, :HW] = ctt[...].T

    @pl.loop(0, D // 256)
    def _(n):
        n0 = pl.multiple_of(n * 256, 256)
        tmp[:, pl.ds(n0, 256)] = nt(du[...], wq[pl.ds(n0, 256), :]).astype(BF)

    ns[...] = tmp[...].reshape(NSEQ, 2, D)
    send_all(ns, nr, 3)

    arrived(cs, cr, 2)
    gc[...] = nn(unmix, cr[...].reshape(R, HW)).astype(BF)

    @pl.loop(0, D // 256)
    def _(n):
        n0 = pl.multiple_of(n * 256, 256)
        part = nn(gc[...], wo[:, pl.ds(n0, 256)]).astype(BF).astype(F32)
        tokn = tokv[:, pl.ds(n0, 256)].astype(F32)
        for s in range(2):
            xf = jnp.where(hcol[s] > 0.5, tokn, xv[s, :, pl.ds(n0, 256)].astype(F32))
            outv[s, :, pl.ds(n0, 256)] = (xf + part[s * L : (s + 1) * L]).astype(BF)

    out_copy = pltpu.make_async_copy(outv, out_hbm.at[0], out_sem.at[0])
    out_copy.start()

    arrived(ns, nr, 3)
    xn[...] = nr[...].reshape(R, D)

    @pl.loop(0, D // 256)
    def _(n):
        n0 = pl.multiple_of(n * 256, 256)
        tmp[:, pl.ds(n0, 256)] = nn(unmix, xn[:, pl.ds(n0, 256)]).astype(BF)

    a0[...] = jnp.zeros_like(a0)

    def finish_step(i, sums):
        token_sum, gain_sum = sums
        s = i // 8
        f0 = pl.multiple_of((i % 8) * XY, XY)
        r0 = pl.multiple_of(i * XY, XY)
        h = hcol[s, pl.ds(f0, XY), :] > 0.5
        rinv = rcol[s, pl.ds(f0, XY), :]
        xu = jnp.where(h, tok, xv[s, pl.ds(f0, XY), :].astype(F32)) * rinv
        gn = tmp[pl.ds(r0, XY), :].astype(F32)
        g = gn * gain
        mean = jnp.mean(g * xu, axis=1, keepdims=True)
        gi = cotv[s, pl.ds(f0, XY), :].astype(F32) + (g - xu * mean) * rinv
        gxv[s, pl.ds(f0, XY), :] = jnp.where(h, 0.0, gi).astype(BF)
        ht = jnp.where(h, gi, 0.0)
        gx = gn * xu
        return token_sum + ht[:8] + ht[8:], gain_sum + gx[:8] + gx[8:]

    zero = jnp.zeros((8, D), F32)
    token_sum, gain_sum = lax.fori_loop(0, 16, finish_step, (zero, zero))
    gx_copy = pltpu.make_async_copy(gxv, gx_hbm.at[0], out_sem.at[1])
    gx_copy.start()
    token_sum = jnp.sum(token_sum, axis=0, keepdims=True)
    gain_sum = jnp.sum(gain_sum, axis=0, keepdims=True)
    coef_col = jnp.sum(coefs[...], axis=1, keepdims=True)
    coef_row = jnp.sum(
        jnp.where(iota((16, 128), 0) == iota((16, 128), 1), coef_col, 0.0), axis=0, keepdims=True
    )
    for c in range(12):
        a0[c // 2, pl.ds(c % 2, 1), :] = token_sum[:, c * 128 : (c + 1) * 128]
        a0[6 + c // 2, pl.ds(c % 2, 1), :] = gain_sum[:, c * 128 : (c + 1) * 128]
    a0[12, pl.ds(0, 1), :] = coef_row

    def small(src, dst, phase, to):
        return pltpu.make_async_remote_copy(
            src_ref=src,
            dst_ref=dst,
            send_sem=send_sem.at[phase],
            recv_sem=recv_sem.at[phase],
            device_id=to,
            device_id_type=MESH,
        )

    def drain15(ref, sem):
        part = ref.at[pl.ds(0, 15)]
        pltpu.make_async_copy(part, part, sem).wait()

    b1[pl.ds(yx, 1)] = a0[pl.ds(yx, 1)]

    def scatter(k, _):
        t = (yx + k) % XY
        small(a0.at[t], b1.at[yx], 4, {"seq": z * XY + t}).start()
        return 0

    lax.fori_loop(1, XY, scatter, 0)
    drain15(b1, recv_sem.at[4])
    zc = z * 2 + core
    b2[pl.ds(zc, 1)] = jnp.sum(b1[...], axis=0, keepdims=True)

    def across(k, _):
        t = (zc + k) % XY
        small(b2.at[zc], b2.at[zc], 5, {"dp": t % 2, "seq": (t // 2) * XY + yx}).start()
        return 0

    lax.fori_loop(1, XY, across, 0)
    drain15(b2, recv_sem.at[5])
    b3[pl.ds(yx, 1)] = jnp.sum(b2[...], axis=0, keepdims=True)

    def gather(k, _):
        t = (yx + k) % XY
        small(b3.at[yx], b3.at[yx], 6, {"seq": z * XY + t}).start()
        return 0

    lax.fori_loop(1, XY, gather, 0)
    drain15(b3, recv_sem.at[6])
    for c in range(12):
        token_ref[:, c * 128 : (c + 1) * 128] = b3[c // 2, pl.ds(c % 2, 1), :]
        gain_out_ref[:, c * 128 : (c + 1) * 128] = b3[6 + c // 2, pl.ds(c % 2, 1), :]
    coef_out_ref[...] = b3[12, pl.ds(0, 1), :]

    drain(xs, send_sem.at[0])
    drain(gs, send_sem.at[1])
    drain(cs, send_sem.at[2])
    drain(ns, send_sem.at[3])
    for phase, ref in ((4, a0), (5, b2), (6, b3)):
        drain15(ref, send_sem.at[phase])
    out_copy.wait()
    gx_copy.wait()


def on_device(
    joints_x,
    cotangent,
    hidden,
    stream_clip,
    stream_kind,
    adjacency,
    mask_token,
    norm_gain,
    w_qkv,
    w_out,
    graph_coef,
):
    any_space = pl.BlockSpec(memory_space=pl.ANY)
    vmem = pl.BlockSpec(memory_space=pltpu.VMEM)
    smem = pl.BlockSpec(memory_space=pltpu.SMEM)
    dma = pltpu.SemaphoreType.DMA
    S = jax.ShapeDtypeStruct
    outs = pl.pallas_call(
        fused_kernel,
        out_shape=(
            S((1, 2, L, D), BF),
            S((1, 2, L, D), BF),
            S((1, D), F32),
            S((1, D), F32),
            S((1, 128), F32),
        ),
        in_specs=[any_space] * 10 + [smem],
        out_specs=(any_space, any_space, vmem, vmem, vmem),
        scratch_shapes=[
            pltpu.VMEM((2, L, D), BF),
            pltpu.VMEM((2, L, D), BF),
            pltpu.VMEM((1, 2, L), jnp.int32),
            pltpu.VMEM((1, R), jnp.int32),
            pltpu.VMEM((1, R), jnp.int32),
            pltpu.VMEM((KINDS, JM, JM), jnp.int32),
            pltpu.VMEM((1, D), BF),
            pltpu.VMEM((1, D), F32),
            pltpu.VMEM((D, 3 * HW), BF),
            pltpu.VMEM((HW, D), BF),
            pltpu.VMEM((2, L, D), BF),
            pltpu.VMEM((2, L, D), BF),
            pltpu.VMEM((NSEQ, 2, D), BF),
            pltpu.VMEM((NSEQ, 2, D), BF),
            pltpu.VMEM((NSEQ, 2, HW), BF),
            pltpu.VMEM((NSEQ, 2, HW), BF),
            pltpu.VMEM((NSEQ, 2, HW), BF),
            pltpu.VMEM((NSEQ, 2, HW), BF),
            pltpu.VMEM((NSEQ, 2, D), BF),
            pltpu.VMEM((NSEQ, 2, D), BF),
            pltpu.VMEM((2, L, 1), F32),
            pltpu.VMEM((2, L, 1), F32),
            pltpu.VMEM((R, 3 * HW), BF),
            pltpu.VMEM((R, D), BF),
            pltpu.VMEM((R, HW), BF),
            pltpu.VMEM((HW, R), BF),
            pltpu.VMEM((HW, R), BF),
            pltpu.VMEM((HW, R), BF),
            pltpu.VMEM((HEADS, R, R), F32),
            pltpu.VMEM((R, 3 * HW), BF),
            pltpu.VMEM((R, R), F32),
            pltpu.VMEM((R, R), F32),
            pltpu.VMEM((16, R), F32),
            pltpu.VMEM((R, D), BF),
            pltpu.VMEM((16, 2, 128), F32),
            pltpu.VMEM((16, 2, 128), F32),
            pltpu.VMEM((16, 2, 128), F32),
            pltpu.VMEM((16, 2, 128), F32),
            dma((10,)),
            dma((7,)),
            dma((7,)),
            dma((4,)),
            dma((2,)),
        ],
        compiler_params=pltpu.CompilerParams(
            collective_id=0, has_side_effects=True, vmem_limit_bytes=60 << 20
        ),
    )(
        joints_x,
        cotangent,
        hidden,
        stream_clip,
        stream_kind,
        adjacency,
        mask_token.reshape(1, D),
        norm_gain.reshape(1, D),
        w_qkv,
        w_out,
        graph_coef,
    )
    layer_out, grad_x, token, gain, coef = outs
    return (layer_out, grad_x, token.reshape(D), gain.reshape(D), coef[0, :HEADS])


def solution(mesh):
    return jax.shard_map(
        on_device,
        mesh=mesh,
        in_specs=(
            P("dp", "seq", None, None),
            P("dp", "seq", None, None),
            P("dp", "seq", None),
            P("dp", None),
            P("dp", None),
            P(),
            P(),
            P(),
            P(),
            P(),
            P(),
        ),
        out_specs=(P("dp", "seq", None, None), P("dp", "seq", None, None), P(), P(), P()),
        check_vma=False,
    )
```

```python
import functools

import jax
import jax.numpy as jnp
from jax import lax
from jax.experimental import pallas as pl
from jax.experimental.pallas import tpu as pltpu
from jax.sharding import PartitionSpec as P

MESH = pl.DeviceIdType.MESH
BF = jnp.bfloat16
F32 = jnp.float32
NSEQ = 128
XY = 16
NZ = 8
D = 1536
HW = 768
HEADS = 12
HD = 64
R = 256
L = 128
KINDS = 4
JM = 136
PAIRS = HEADS // 2
MARK = 1000.0


def iota(shape, axis):
    return lax.broadcasted_iota(jnp.int32, shape, axis)


def nn(a, b):
    return jnp.dot(a, b, preferred_element_type=F32)


def nt(a, b):
    return lax.dot_general(a, b, (((1,), (1,)), ((), ())), preferred_element_type=F32)


def to_column(row, n):
    diag = iota((n, n), 0) == iota((n, n), 1)
    return jnp.sum(jnp.where(diag, row, jnp.zeros_like(row)), axis=1, keepdims=True)


def fused_kernel(
    x_hbm,
    cot_hbm,
    hid_hbm,
    clip_hbm,
    kind_hbm,
    adj_hbm,
    tok_hbm,
    gain_hbm,
    wqkv_hbm,
    wout_hbm,
    coef_ref,
    outv,
    gxv,
    token_ref,
    gain_out_ref,
    coef_out_ref,
    xv,
    cotv,
    hidv,
    clipv,
    kindv,
    adjv,
    tokv,
    gainv,
    wq,
    wo,
    xs,
    xr,
    gs,
    gr,
    cs,
    cr,
    ns,
    nr,
    hcol,
    rcol,
    qkv,
    xn,
    gc,
    vt,
    kt,
    ctt,
    pts,
    du,
    link,
    neg,
    coefs,
    sums,
    tmp,
    a0,
    b1,
    b2,
    b3,
    in_sem,
    send_sem,
    recv_sem,
    loc_sem,
    plane_sem,
):
    me = lax.axis_index("seq")
    core = lax.axis_index("dp")
    z = me // XY
    yx = me % XY
    y = yx // 4
    x = yx % 4

    loads = [
        (x_hbm.at[0], xv),
        (hid_hbm, hidv),
        (tok_hbm, tokv),
        (gain_hbm, gainv),
        (cot_hbm.at[0], cotv),
        (wout_hbm, wo),
        (clip_hbm, clipv),
        (kind_hbm, kindv),
        (adj_hbm, adjv),
        (wqkv_hbm, wq),
    ]
    load = [pltpu.make_async_copy(s, d, in_sem.at[i]) for i, (s, d) in enumerate(loads)]
    for c in load:
        c.start()

    barrier = pltpu.get_barrier_semaphore()

    def greet(k, _):
        pl.semaphore_signal(
            barrier, inc=1, device_id={"seq": (me + k) % NSEQ}, device_id_type=MESH
        )
        return 0

    lax.fori_loop(1, NSEQ, greet, 0)

    def greet_other(k, _):
        pl.semaphore_signal(
            barrier,
            inc=1,
            device_id={"dp": 1 - core, "seq": k * XY + yx},
            device_id_type=MESH,
        )
        return 0

    lax.fori_loop(0, NZ, greet_other, 0)

    for c in load[:4]:
        c.wait()
    tok = tokv[...].astype(F32)
    gain = gainv[...]
    hid = hidv[0].astype(F32)
    for s in range(2):
        hcol[s] = to_column(hid[s : s + 1, :], L)
    def peer(dz, dyx):
        return ((z + dz) % NZ) * XY + ((y + dyx // 4) % 4) * 4 + (x + dyx % 4) % 4

    def send(src, dst, phase, to):
        return pltpu.make_async_remote_copy(
            src_ref=src,
            dst_ref=dst,
            send_sem=send_sem.at[phase],
            recv_sem=recv_sem.at[phase],
            device_id={"seq": to},
            device_id_type=MESH,
        )

    def send_all(src, dst, phase):
        pltpu.make_async_copy(src.at[me], dst.at[me], loc_sem.at[phase]).start()

        def body(k, _):
            to = peer(k % NZ, k // NZ)
            send(src.at[to], dst.at[me], phase, to).start()
            return 0

        lax.fori_loop(1, NSEQ, body, 0)

    def drain(ref, sem):
        part = ref.at[pl.ds(0, NSEQ - 1)]
        pltpu.make_async_copy(part, part, sem).wait()

    def arrived(src, dst, phase):
        pltpu.make_async_copy(src.at[me], dst.at[me], loc_sem.at[phase]).wait()
        drain(dst, recv_sem.at[phase])

    r32, c32 = iota((32, 32), 0), iota((32, 32), 1)
    mix32 = (c32 == (r32 % 2) * 16 + r32 // 2).astype(BF)

    def offset(i):
        near = i // 2 + 1
        return jnp.where(i == NZ - 1, 0, jnp.where(i % 2 == 1, NZ - near, near))

    def norm_step(i, _):
        zz = (z + offset(i)) % NZ
        f0 = pl.multiple_of(zz * XY, XY)
        parts = []
        for s in range(2):
            xf = xv[s, pl.ds(f0, XY), :].astype(F32)
            h = hcol[s, pl.ds(f0, XY), :]
            xf = jnp.where(h > 0.5, tok, xf)
            rinv = 1.0 / jnp.sqrt(jnp.mean(xf * xf, axis=1, keepdims=True) + 1e-06)
            rcol[s, pl.ds(f0, XY), :] = rinv
            row = xf * rinv * gain
            mark = (h > 0.5) & (iota((XY, D), 1) == 0)
            parts.append(jnp.where(mark, MARK, row).astype(BF))
        both = nn(mix32, jnp.concatenate(parts, axis=0)).astype(BF)
        xs[pl.ds(f0, XY)] = both.reshape(XY, 2, D)

        @pl.when(i == 0)
        def _():
            pl.semaphore_wait(barrier, NSEQ - 1 + NZ)

        def body(k, _):
            to = zz * XY + ((y + k // 4) % 4) * 4 + (x + k % 4) % 4

            @pl.when(to != me)
            def _():
                send(xs.at[to], xr.at[me], 0, to).start()

            return 0

        lax.fori_loop(0, XY, body, 0)
        return 0

    lax.fori_loop(0, NZ, norm_step, 0)
    pltpu.make_async_copy(xs.at[me], xr.at[me], loc_sem.at[0]).start()

    ri, ci = iota((R, R), 0), iota((R, R), 1)
    mix = (ci == (ri % 2) * L + ri // 2).astype(BF)
    unmix = (ci == (ri % L) * 2 + ri // L).astype(BF)
    unmix32 = (c32 == (r32 % XY) * 2 + r32 // XY).astype(BF)
    for c in load[4:6]:
        c.wait()

    @pl.loop(0, HW // 256)
    def _(n):
        n0 = pl.multiple_of(n * 256, 256)
        part = nt(cotv[...].reshape(R, D), wo[pl.ds(n0, 256), :]).astype(BF)
        tmp[:, pl.ds(n0, 256)] = nn(mix, part).astype(BF)

    gs[...] = tmp[:, :HW].reshape(NSEQ, 2, HW)
    scot = jnp.zeros((8, D), F32)
    for s in range(2):
        picks = jnp.broadcast_to(hid[s : s + 1, :], (8, L)).astype(BF)
        scot = scot + nn(picks, cotv[s])
    sums[0:1, :] = scot[0:1]
    drain(xs, send_sem.at[0])
    send_all(gs, gr, 1)

    for c in load[6:9]:
        c.wait()
    clip_row = clipv[...]
    clip_col = to_column(clip_row, R)
    same = clip_col == clip_row
    first_row = jnp.min(jnp.where(same, ri, R), axis=0, keepdims=True)
    first_col = to_column(first_row, R)
    kind_col = to_column(kindv[...], R)
    joint_col = iota((R, 1), 0) - first_col
    pick = iota((R, JM), 1) == joint_col
    picked = jnp.zeros((R, JM), F32)
    for k in range(KINDS):
        rows = (pick & (kind_col == k)).astype(BF)
        picked = picked + nn(rows, adjv[k].astype(F32).astype(BF))
    link[...] = nt(pick.astype(BF), picked.astype(BF))
    neg[...] = jnp.where(same, jnp.float32(0.0), -jnp.inf)

    load[9].wait()
    arrived(xs, xr, 0)
    xn[...] = xr[...].reshape(R, D)
    head = xn[:, :128]
    flag_col = jnp.where(head[:, 0:1].astype(F32) > MARK / 2, 1.0, 0.0)
    flag_row = jnp.sum(jnp.where(ri == ci, flag_col, 0.0), axis=0, keepdims=True)
    flags = jnp.broadcast_to(flag_row, (8, R)).astype(BF)
    tok_rinv = 1.0 / jnp.sqrt(jnp.mean(tok * tok, axis=1, keepdims=True) + 1e-06)
    tok_unit = tok * tok_rinv
    tok_head = (tok_unit * gain)[:, :128].astype(BF).astype(F32)
    fix = (flag_col > 0.5) & (iota((R, 128), 1) == 0)
    xn[:, :128] = jnp.where(fix, tok_head, head.astype(F32)).astype(BF)

    @pl.loop(0, 3 * HW // 256)
    def _(n):
        n0 = pl.multiple_of(n * 256, 256)
        part = nn(xn[...], wq[:, pl.ds(n0, 256)]).astype(BF)
        scale = jnp.where(n < HW // 256, HD**-0.5, 1.0).astype(BF)
        qkv[:, pl.ds(n0, 256)] = part * scale

    coefs[...] = jnp.zeros_like(coefs)
    kt[...] = qkv[:, HW : 2 * HW].T
    vt[...] = qkv[:, 2 * HW :].T

    lane = iota((R, 128), 1)

    @pl.loop(0, PAIRS)
    def _(j):
        c0 = pl.multiple_of(j * 128, 128)
        q2 = qkv[:, pl.ds(c0, 128)]
        k2 = qkv[:, pl.ds(HW + c0, 128)]
        for i in range(2):
            h = j * 2 + i
            kh = jnp.where((lane < HD) == (i == 0), k2, jnp.zeros_like(k2))
            st = nt(kh, q2) + (coef_ref[h] * link[...] + neg[...])
            e = jnp.exp(st - jnp.max(st, axis=0, keepdims=True))
            pt = e * (1.0 / jnp.sum(e, axis=0, keepdims=True))
            pts[h] = pt
            r0 = pl.multiple_of(h * HD, HD)
            ctt[pl.ds(r0, HD), :] = nn(vt[pl.ds(r0, HD), :], pt.astype(BF)).astype(BF)

    cs[...] = ctt[...].T.reshape(NSEQ, 2, HW)
    send_all(cs, cr, 2)

    arrived(gs, gr, 1)
    gc[...] = gr[...].reshape(R, HW)

    @pl.loop(0, PAIRS)
    def _(j):
        c0 = pl.multiple_of(j * 128, 128)
        q2 = qkv[:, pl.ds(c0, 128)]
        v2 = qkv[:, pl.ds(2 * HW + c0, 128)]
        g2 = gc[:, pl.ds(c0, 128)]
        dk, dv = [], []
        for i in range(2):
            h = j * 2 + i
            vh = jnp.where((lane < HD) == (i == 0), v2, jnp.zeros_like(v2))
            dp = nt(vh, g2)
            pt = pts[h]
            ds = pt * (dp - jnp.sum(pt * dp, axis=0, keepdims=True))
            coefs[pl.ds(h, 1), :] = jnp.sum(ds * link[...], axis=0, keepdims=True)
            db = ds.astype(BF)
            r0 = pl.multiple_of(h * HD, HD)
            dq = nn(kt[pl.ds(r0, HD), :], db) * (HD**-0.5)
            ctt[pl.ds(r0, HD), :] = dq.astype(BF)
            dk.append(nn(db, q2))
            dv.append(nn(pt.astype(BF), g2))
        du[:, pl.ds(HW + c0, 128)] = jnp.where(lane < HD, dk[0], dk[1]).astype(BF)
        du[:, pl.ds(2 * HW + c0, 128)] = jnp.where(lane < HD, dv[0], dv[1]).astype(BF)

    du[:, :HW] = ctt[...].T

    @pl.loop(0, D // 256)
    def _(n):
        n0 = pl.multiple_of(n * 256, 256)
        gn = nt(du[...], wq[pl.ds(n0, 256), :]).astype(BF)
        tmp[:, pl.ds(n0, 256)] = gn
        sums[1:2, pl.ds(n0, 256)] = nn(flags, gn)[0:1]
        prod = gn.astype(F32) * xn[:, pl.ds(n0, 256)].astype(F32)
        sums[2:3, pl.ds(n0, 256)] = jnp.sum(prod, axis=0, keepdims=True)

    sgn = gain * sums[1:2, :]
    token_sum = sgn - tok_unit * jnp.mean(sgn * tok_unit, axis=1, keepdims=True)
    token_sum = sums[0:1, :] + token_sum * tok_rinv
    gain_sum = sums[2:3, :] / gain
    coef_col = jnp.sum(coefs[...], axis=1, keepdims=True)
    coef_row = jnp.sum(
        jnp.where(iota((16, 128), 0) == iota((16, 128), 1), coef_col, 0.0), axis=0, keepdims=True
    )
    a0[...] = jnp.zeros_like(a0)
    for c in range(12):
        a0[c // 2, pl.ds(c % 2, 1), :] = token_sum[:, c * 128 : (c + 1) * 128]
        a0[6 + c // 2, pl.ds(c % 2, 1), :] = gain_sum[:, c * 128 : (c + 1) * 128]
    a0[12, pl.ds(0, 1), :] = coef_row

    def small(src, dst, phase, to):
        return pltpu.make_async_remote_copy(
            src_ref=src,
            dst_ref=dst,
            send_sem=send_sem.at[phase],
            recv_sem=recv_sem.at[phase],
            device_id=to,
            device_id_type=MESH,
        )

    def drain15(ref, sem):
        part = ref.at[pl.ds(0, 15)]
        pltpu.make_async_copy(part, part, sem).wait()

    b1[pl.ds(yx, 1)] = a0[pl.ds(yx, 1)]

    def scatter(k, _):
        t = (yx + k) % XY
        small(a0.at[t], b1.at[yx], 4, {"seq": z * XY + t}).start()
        return 0

    lax.fori_loop(1, XY, scatter, 0)

    ns[...] = tmp[...].reshape(NSEQ, 2, D)

    def send_plane(i, _):
        dz = offset(i)

        def body(k, _):
            to = peer(dz, k)

            @pl.when(to != me)
            def _():
                pltpu.make_async_remote_copy(
                    src_ref=ns.at[to],
                    dst_ref=nr.at[me],
                    send_sem=send_sem.at[3],
                    recv_sem=plane_sem.at[dz],
                    device_id={"seq": to},
                    device_id_type=MESH,
                ).start()

            return 0

        lax.fori_loop(0, XY, body, 0)
        return 0

    lax.fori_loop(0, NZ, send_plane, 0)
    pltpu.make_async_copy(ns.at[me], nr.at[me], plane_sem.at[0]).start()

    drain15(b1, recv_sem.at[4])
    zc = z * 2 + core
    b2[pl.ds(zc, 1)] = jnp.sum(b1[...], axis=0, keepdims=True)

    def across(k, _):
        t = (zc + k) % XY
        small(b2.at[zc], b2.at[zc], 5, {"dp": t % 2, "seq": (t // 2) * XY + yx}).start()
        return 0

    lax.fori_loop(1, XY, across, 0)

    arrived(cs, cr, 2)
    gc[...] = nn(unmix, cr[...].reshape(R, HW)).astype(BF)

    @pl.loop(0, D // 256)
    def _(n):
        n0 = pl.multiple_of(n * 256, 256)
        part = nn(gc[...], wo[:, pl.ds(n0, 256)]).astype(BF).astype(F32)
        tokn = tokv[:, pl.ds(n0, 256)].astype(F32)
        for s in range(2):
            xf = jnp.where(hcol[s] > 0.5, tokn, xv[s, :, pl.ds(n0, 256)].astype(F32))
            outv[0, s, :, pl.ds(n0, 256)] = (xf + part[s * L : (s + 1) * L]).astype(BF)

    drain15(b2, recv_sem.at[5])
    b3[pl.ds(yx, 1)] = jnp.sum(b2[...], axis=0, keepdims=True)

    def gather(k, _):
        t = (yx + k) % XY
        small(b3.at[yx], b3.at[yx], 6, {"seq": z * XY + t}).start()
        return 0

    lax.fori_loop(1, XY, gather, 0)

    def finish_step(i, _):
        dz = offset(i)
        f0 = pl.multiple_of(((z + NZ - dz) % NZ) * XY, XY)
        block = nr.at[pl.ds(f0, XY)]
        pltpu.make_async_copy(block, block, plane_sem.at[dz]).wait()
        both = nn(unmix32, nr[pl.ds(f0, XY)].reshape(2 * XY, D))
        for s in range(2):
            h = hcol[s, pl.ds(f0, XY), :] > 0.5
            rinv = rcol[s, pl.ds(f0, XY), :]
            xu = jnp.where(h, tok, xv[s, pl.ds(f0, XY), :].astype(F32)) * rinv
            g = both[s * XY : (s + 1) * XY] * gain
            mean = jnp.mean(g * xu, axis=1, keepdims=True)
            gi = cotv[s, pl.ds(f0, XY), :].astype(F32) + (g - xu * mean) * rinv
            gxv[0, s, pl.ds(f0, XY), :] = jnp.where(h, 0.0, gi).astype(BF)
        return 0

    lax.fori_loop(0, NZ, finish_step, 0)

    drain15(b3, recv_sem.at[6])
    for c in range(12):
        token_ref[:, c * 128 : (c + 1) * 128] = b3[c // 2, pl.ds(c % 2, 1), :]
        gain_out_ref[:, c * 128 : (c + 1) * 128] = b3[6 + c // 2, pl.ds(c % 2, 1), :]
    coef_out_ref[...] = b3[12, pl.ds(0, 1), :]

    drain(gs, send_sem.at[1])
    drain(cs, send_sem.at[2])
    drain(ns, send_sem.at[3])
    for phase, ref in ((4, a0), (5, b2), (6, b3)):
        drain15(ref, send_sem.at[phase])


def place_kernel(out_in, gx_in, token_in, gain_in, coef_in, out, gx, token, gain, coef, sem):
    copies = [
        pltpu.make_async_copy(out_in, out, sem.at[0]),
        pltpu.make_async_copy(gx_in, gx, sem.at[1]),
    ]
    for c in copies:
        c.start()
    token[...] = token_in[...].reshape(D)
    gain[...] = gain_in[...].reshape(D)
    coef[...] = coef_in[...].reshape(128)[:HEADS]
    for c in copies:
        c.wait()


def on_device(
    joints_x,
    cotangent,
    hidden,
    stream_clip,
    stream_kind,
    adjacency,
    mask_token,
    norm_gain,
    w_qkv,
    w_out,
    graph_coef,
):
    any_space = pl.BlockSpec(memory_space=pl.ANY)
    vmem = pl.BlockSpec(memory_space=pltpu.VMEM)
    smem = pl.BlockSpec(memory_space=pltpu.SMEM)
    dma = pltpu.SemaphoreType.DMA
    S = jax.ShapeDtypeStruct
    outs = pl.pallas_call(
        fused_kernel,
        out_shape=(
            S((1, 2, L, D), BF),
            S((1, 2, L, D), BF),
            S((1, D), F32),
            S((1, D), F32),
            S((1, 128), F32),
        ),
        in_specs=[any_space] * 10 + [smem],
        out_specs=(vmem,) * 5,
        scratch_shapes=[
            pltpu.VMEM((2, L, D), BF),
            pltpu.VMEM((2, L, D), BF),
            pltpu.VMEM((1, 2, L), jnp.int32),
            pltpu.VMEM((1, R), jnp.int32),
            pltpu.VMEM((1, R), jnp.int32),
            pltpu.VMEM((KINDS, JM, JM), jnp.int32),
            pltpu.VMEM((1, D), BF),
            pltpu.VMEM((1, D), F32),
            pltpu.VMEM((D, 3 * HW), BF),
            pltpu.VMEM((HW, D), BF),
            pltpu.VMEM((NSEQ, 2, D), BF),
            pltpu.VMEM((NSEQ, 2, D), BF),
            pltpu.VMEM((NSEQ, 2, HW), BF),
            pltpu.VMEM((NSEQ, 2, HW), BF),
            pltpu.VMEM((NSEQ, 2, HW), BF),
            pltpu.VMEM((NSEQ, 2, HW), BF),
            pltpu.VMEM((NSEQ, 2, D), BF),
            pltpu.VMEM((NSEQ, 2, D), BF),
            pltpu.VMEM((2, L, 1), F32),
            pltpu.VMEM((2, L, 1), F32),
            pltpu.VMEM((R, 3 * HW), BF),
            pltpu.VMEM((R, D), BF),
            pltpu.VMEM((R, HW), BF),
            pltpu.VMEM((HW, R), BF),
            pltpu.VMEM((HW, R), BF),
            pltpu.VMEM((HW, R), BF),
            pltpu.VMEM((HEADS, R, R), F32),
            pltpu.VMEM((R, 3 * HW), BF),
            pltpu.VMEM((R, R), F32),
            pltpu.VMEM((R, R), F32),
            pltpu.VMEM((16, R), F32),
            pltpu.VMEM((8, D), F32),
            pltpu.VMEM((R, D), BF),
            pltpu.VMEM((16, 2, 128), F32),
            pltpu.VMEM((16, 2, 128), F32),
            pltpu.VMEM((16, 2, 128), F32),
            pltpu.VMEM((16, 2, 128), F32),
            dma((10,)),
            dma((7,)),
            dma((7,)),
            dma((4,)),
            dma((NZ,)),
        ],
        compiler_params=pltpu.CompilerParams(
            collective_id=0, has_side_effects=True, vmem_limit_bytes=60 << 20
        ),
    )(
        joints_x,
        cotangent,
        hidden,
        stream_clip,
        stream_kind,
        adjacency,
        mask_token.reshape(1, D),
        norm_gain.reshape(1, D),
        w_qkv,
        w_out,
        graph_coef,
    )
    return pl.pallas_call(
        place_kernel,
        out_shape=(
            S((1, 2, L, D), BF),
            S((1, 2, L, D), BF),
            S((D,), F32),
            S((D,), F32),
            S((HEADS,), F32),
        ),
        in_specs=[vmem] * 5,
        out_specs=(any_space, any_space, vmem, vmem, vmem),
        scratch_shapes=[dma((2,))],
    )(*outs)


def solution(mesh):
    return jax.shard_map(
        on_device,
        mesh=mesh,
        in_specs=(
            P("dp", "seq", None, None),
            P("dp", "seq", None, None),
            P("dp", "seq", None),
            P("dp", None),
            P("dp", None),
            P(),
            P(),
            P(),
            P(),
            P(),
            P(),
        ),
        out_specs=(P("dp", "seq", None, None), P("dp", "seq", None, None), P(), P(), P()),
        check_vma=False,
    )
```

```python
import functools

import jax
import jax.numpy as jnp
from jax import lax
from jax.experimental import pallas as pl
from jax.experimental.pallas import tpu as pltpu
from jax.sharding import PartitionSpec as P

MESH = pl.DeviceIdType.MESH
BF = jnp.bfloat16
F32 = jnp.float32
NSEQ = 128
XY = 16
NZ = 8
D = 1536
HW = 768
HEADS = 12
HD = 64
R = 256
L = 128
KINDS = 4
JM = 136
PAIRS = HEADS // 2
MARK = 1000.0


def iota(shape, axis):
    return lax.broadcasted_iota(jnp.int32, shape, axis)


def nn(a, b):
    return jnp.dot(a, b, preferred_element_type=F32)


def nt(a, b):
    return lax.dot_general(a, b, (((1,), (1,)), ((), ())), preferred_element_type=F32)


def to_column(row, n):
    diag = iota((n, n), 0) == iota((n, n), 1)
    return jnp.sum(jnp.where(diag, row, jnp.zeros_like(row)), axis=1, keepdims=True)


def fused_kernel(
    x_hbm,
    cot_hbm,
    hid_hbm,
    clip_hbm,
    kind_hbm,
    adj_hbm,
    tok_hbm,
    gain_hbm,
    wqkv_hbm,
    wout_hbm,
    coef_ref,
    out_hbm,
    gx_hbm,
    token_ref,
    gain_out_ref,
    coef_out_ref,
    xv,
    cotv,
    hidv,
    clipv,
    kindv,
    adjv,
    tokv,
    gainv,
    wq,
    wo,
    outv,
    gxv,
    xs,
    xr,
    gs,
    gr,
    cs,
    cr,
    ns,
    nr,
    ns2,
    nr2,
    hcol,
    rcol,
    qkv,
    xn,
    gc,
    vt,
    kt,
    ctt,
    dqt,
    pts,
    invs,
    du,
    link,
    bias,
    coefs,
    sums,
    tmp,
    a0,
    b1,
    b2,
    b3,
    in_sem,
    send_sem,
    recv_sem,
    loc_sem,
    plane_sem,
    out_sem,
):
    me = lax.axis_index("seq")
    core = lax.axis_index("dp")
    z = me // XY
    yx = me % XY
    y = yx // 4
    x = yx % 4

    loads = [
        (x_hbm.at[0], xv),
        (hid_hbm, hidv),
        (tok_hbm, tokv),
        (gain_hbm, gainv),
        (cot_hbm.at[0], cotv),
        (wout_hbm, wo),
        (clip_hbm, clipv),
        (kind_hbm, kindv),
        (adj_hbm, adjv),
        (wqkv_hbm, wq),
    ]
    load = [pltpu.make_async_copy(s, d, in_sem.at[i]) for i, (s, d) in enumerate(loads)]
    for c in load:
        c.start()

    barrier = pltpu.get_barrier_semaphore()

    def greet(k, _):
        pl.semaphore_signal(
            barrier, inc=1, device_id={"seq": (me + k) % NSEQ}, device_id_type=MESH
        )
        return 0

    lax.fori_loop(1, NSEQ, greet, 0)

    def greet_other(k, _):
        pl.semaphore_signal(
            barrier,
            inc=1,
            device_id={"dp": 1 - core, "seq": k * XY + yx},
            device_id_type=MESH,
        )
        return 0

    lax.fori_loop(0, NZ, greet_other, 0)

    for c in load[:4]:
        c.wait()
    tok = tokv[...].astype(F32).reshape(1, D)
    gain = gainv[...].reshape(1, D)
    sums[3:4, :] = tok
    hid = hidv[0].astype(F32)
    for s in range(2):
        hcol[s] = to_column(hid[s : s + 1, :], L)
    def peer(dz, dyx):
        return ((z + dz) % NZ) * XY + ((y + dyx // 4) % 4) * 4 + (x + dyx % 4) % 4

    def send(src, dst, phase, to):
        return pltpu.make_async_remote_copy(
            src_ref=src,
            dst_ref=dst,
            send_sem=send_sem.at[phase],
            recv_sem=recv_sem.at[phase],
            device_id={"seq": to},
            device_id_type=MESH,
        )

    def send_all(src, dst, phase):
        pltpu.make_async_copy(src.at[me], dst.at[me], loc_sem.at[phase]).start()

        def body(k, _):
            to = peer(k % NZ, k // NZ)
            send(src.at[to], dst.at[me], phase, to).start()
            return 0

        lax.fori_loop(1, NSEQ, body, 0)

    def drain(ref, sem):
        part = ref.at[pl.ds(0, NSEQ - 1)]
        pltpu.make_async_copy(part, part, sem).wait()

    def arrived(src, dst, phase):
        pltpu.make_async_copy(src.at[me], dst.at[me], loc_sem.at[phase]).wait()
        drain(dst, recv_sem.at[phase])

    r32, c32 = iota((32, 32), 0), iota((32, 32), 1)
    mix32 = (c32 == (r32 % 2) * 16 + r32 // 2).astype(BF)

    def offset(i):
        near = i // 2 + 1
        return jnp.where(i == NZ - 1, 0, jnp.where(i % 2 == 1, NZ - near, near))

    def norm_step(i, _):
        zz = (z + offset(i)) % NZ
        f0 = pl.multiple_of(zz * XY, XY)
        parts = []
        for s in range(2):
            xf = xv[s, pl.ds(f0, XY), :].astype(F32)
            h = hcol[s, pl.ds(f0, XY), :]
            xf = jnp.where(h > 0.5, tok, xf)
            rinv = 1.0 / jnp.sqrt(jnp.mean(xf * xf, axis=1, keepdims=True) + 1e-06)
            rcol[s, pl.ds(f0, XY), :] = rinv
            row = xf * rinv * gain
            mark = (h > 0.5) & (iota((XY, D), 1) == 0)
            parts.append(jnp.where(mark, MARK, row).astype(BF))
        both = nn(mix32, jnp.concatenate(parts, axis=0)).astype(BF)
        xs[pl.ds(f0, XY)] = both.reshape(XY, 2, D)

        @pl.when(i == 0)
        def _():
            pl.semaphore_wait(barrier, NSEQ - 1 + NZ)

        def body(k, _):
            to = zz * XY + ((y + k // 4) % 4) * 4 + (x + k % 4) % 4

            @pl.when(to != me)
            def _():
                send(xs.at[to], xr.at[me], 0, to).start()

            return 0

        lax.fori_loop(0, XY, body, 0)
        return 0

    lax.fori_loop(0, NZ, norm_step, 0)
    pltpu.make_async_copy(xs.at[me], xr.at[me], loc_sem.at[0]).start()

    ri, ci = iota((R, R), 0), iota((R, R), 1)
    mix = (ci == (ri % 2) * L + ri // 2).astype(BF)
    unmix = (ci == (ri % L) * 2 + ri // L).astype(BF)
    unmix32 = (c32 == (r32 % XY) * 2 + r32 // XY).astype(BF)
    for c in load[4:6]:
        c.wait()

    @pl.loop(0, HW // 256, unroll=True)
    def _(n):
        n0 = pl.multiple_of(n * 256, 256)
        part = nt(cotv[...].reshape(R, D), wo[pl.ds(n0, 256), :]).astype(BF)
        tmp[:, pl.ds(n0, 256)] = nn(mix, part).astype(BF)

    gs[...] = tmp[:, :HW].reshape(NSEQ, 2, HW)
    scot = jnp.zeros((8, D), F32)
    for s in range(2):
        picks = jnp.broadcast_to(hid[s : s + 1, :], (8, L)).astype(BF)
        scot = scot + nn(picks, cotv[s])
    sums[0:1, :] = scot[0:1]
    drain(xs, send_sem.at[0])
    send_all(gs, gr, 1)

    for c in load[6:9]:
        c.wait()
    clip_row = clipv[...]
    clip_col = to_column(clip_row, R)
    same = clip_col == clip_row
    first_row = jnp.min(jnp.where(same, ri, R), axis=0, keepdims=True)
    first_col = to_column(first_row, R)
    kind_col = to_column(kindv[...], R)
    joint_col = iota((R, 1), 0) - first_col
    pick = iota((R, JM), 1) == joint_col
    picked = jnp.zeros((R, JM), F32)
    for k in range(KINDS):
        rows = (pick & (kind_col == k)).astype(BF)
        picked = picked + nn(rows, adjv[k].astype(F32).astype(BF))
    link[...] = nt(pick.astype(BF), picked.astype(BF))
    bias[...] = jnp.where(same, link[...], -jnp.inf)

    load[9].wait()
    arrived(xs, xr, 0)
    xn[...] = xr[...].reshape(R, D)
    head = xn[:, :128]
    flag_col = jnp.where(head[:, 0:1].astype(F32) > MARK / 2, 1.0, 0.0)
    flag_row = jnp.sum(jnp.where(ri == ci, flag_col, 0.0), axis=0, keepdims=True)
    flags = jnp.broadcast_to(flag_row, (8, R)).astype(BF)
    tok_rinv = 1.0 / jnp.sqrt(jnp.mean(tok * tok, axis=1, keepdims=True) + 1e-06)
    tok_unit = tok * tok_rinv
    tok_head = (tok_unit * gain)[:, :128].astype(BF).astype(F32)
    fix = (flag_col > 0.5) & (iota((R, 128), 1) == 0)
    xn[:, :128] = jnp.where(fix, tok_head, head.astype(F32)).astype(BF)

    @pl.loop(0, 3 * HW // 256, unroll=True)
    def _(n):
        n0 = pl.multiple_of(n * 256, 256)
        part = nn(xn[...], wq[:, pl.ds(n0, 256)]).astype(BF)
        scale = jnp.where(n < HW // 256, HD**-0.5, 1.0).astype(BF)
        qkv[:, pl.ds(n0, 256)] = part * scale

    coefs[...] = jnp.zeros_like(coefs)
    kt[...] = qkv[:, HW : 2 * HW].T
    vt[...] = qkv[:, 2 * HW :].T

    lane = iota((R, 128), 1)

    @pl.loop(0, PAIRS, unroll=True)
    def _(j):
        c0 = pl.multiple_of(j * 128, 128)
        q2 = qkv[:, pl.ds(c0, 128)]
        k2 = qkv[:, pl.ds(HW + c0, 128)]
        for i in range(2):
            h = j * 2 + i
            r0 = pl.multiple_of(h * HD, HD)
            kh = jnp.where((lane < HD) == (i == 0), k2, jnp.zeros_like(k2))
            rows = []
            for half in range(2):
                cols = slice(half * 128, half * 128 + 128)
                st = nt(kh, q2[cols]) + coef_ref[h] * bias[:, cols]
                e = jnp.exp(st - jnp.max(st, axis=0, keepdims=True))
                inv = 1.0 / jnp.sum(e, axis=0, keepdims=True)
                eb = e.astype(BF)
                pts[h, :, cols] = eb
                rows.append(inv)
                ct = nn(vt[pl.ds(r0, HD), :], eb) * inv
                ctt[pl.ds(r0, HD), cols] = ct.astype(BF)
            invs[pl.ds(h, 1), :] = jnp.concatenate(rows, axis=1)

    cs[...] = ctt[...].T.reshape(NSEQ, 2, HW)
    send_all(cs, cr, 2)

    arrived(gs, gr, 1)
    gc[...] = gr[...].reshape(R, HW)

    @pl.loop(0, PAIRS, unroll=True)
    def _(j):
        c0 = pl.multiple_of(j * 128, 128)
        q2 = qkv[:, pl.ds(c0, 128)]
        v2 = qkv[:, pl.ds(2 * HW + c0, 128)]
        g2 = gc[:, pl.ds(c0, 128)]
        dk, dv = [], []
        for i in range(2):
            h = j * 2 + i
            r0 = pl.multiple_of(h * HD, HD)
            vh = jnp.where((lane < HD) == (i == 0), v2, jnp.zeros_like(v2))
            dbs, pbs, rows = [], [], []
            inv = invs[pl.ds(h, 1), :]
            for half in range(2):
                cols = slice(half * 128, half * 128 + 128)
                p = pts[h, :, cols].astype(F32) * inv[:, cols]
                dp = nt(vh, g2[cols])
                ds = p * (dp - jnp.sum(p * dp, axis=0, keepdims=True))
                rows.append(jnp.sum(ds * link[:, cols], axis=0, keepdims=True))
                db = ds.astype(BF)
                dq = nn(kt[pl.ds(r0, HD), :], db) * (HD**-0.5)
                dqt[pl.ds(r0, HD), cols] = dq.astype(BF)
                dbs.append(db)
                pbs.append(p.astype(BF))
            coefs[pl.ds(h, 1), :] = jnp.concatenate(rows, axis=1)
            dk.append(nn(jnp.concatenate(dbs, axis=1), q2))
            dv.append(nn(jnp.concatenate(pbs, axis=1), g2))
        du[:, pl.ds(HW + c0, 128)] = jnp.where(lane < HD, dk[0], dk[1]).astype(BF)
        du[:, pl.ds(2 * HW + c0, 128)] = jnp.where(lane < HD, dv[0], dv[1]).astype(BF)

    du[:, :HW] = dqt[...].T

    for half, (src, dst) in enumerate(((ns, nr), (ns2, nr2))):

        @pl.loop(0, HW // 256, unroll=True)
        def _(n, half=half):
            n0 = pl.multiple_of(half * HW + n * 256, 256)
            gn = nt(du[...], wq[pl.ds(n0, 256), :]).astype(BF)
            tmp[:, pl.ds(n0, 256)] = gn
            sums[1:2, pl.ds(n0, 256)] = nn(flags, gn)[0:1]
            prod = gn.astype(F32) * xn[:, pl.ds(n0, 256)].astype(F32)
            sums[2:3, pl.ds(n0, 256)] = jnp.sum(prod, axis=0, keepdims=True)

        src[...] = tmp[:, half * HW : half * HW + HW].reshape(NSEQ, 2, HW)

        def send_plane(i, _, src=src, dst=dst, half=half):
            dz = offset(i)

            def body(k, _):
                to = peer(dz, k)

                @pl.when(to != me)
                def _():
                    pltpu.make_async_remote_copy(
                        src_ref=src.at[to],
                        dst_ref=dst.at[me],
                        send_sem=send_sem.at[3 + half * 4],
                        recv_sem=plane_sem.at[half, dz],
                        device_id={"seq": to},
                        device_id_type=MESH,
                    ).start()

                return 0

            lax.fori_loop(0, XY, body, 0)
            return 0

        lax.fori_loop(0, NZ, send_plane, 0)
        pltpu.make_async_copy(src.at[me], dst.at[me], plane_sem.at[half, 0]).start()

    sgn = gain * sums[1:2, :]
    token_sum = sgn - tok_unit * jnp.mean(sgn * tok_unit, axis=1, keepdims=True)
    token_sum = sums[0:1, :] + token_sum * tok_rinv
    gain_sum = sums[2:3, :] / gain
    coef_col = jnp.sum(coefs[...], axis=1, keepdims=True)
    coef_row = jnp.sum(
        jnp.where(iota((16, 128), 0) == iota((16, 128), 1), coef_col, 0.0), axis=0, keepdims=True
    )
    a0[...] = jnp.zeros_like(a0)
    for c in range(12):
        a0[c // 2, pl.ds(c % 2, 1), :] = token_sum[:, c * 128 : (c + 1) * 128]
        a0[6 + c // 2, pl.ds(c % 2, 1), :] = gain_sum[:, c * 128 : (c + 1) * 128]
    a0[12, pl.ds(0, 1), :] = coef_row

    def small(src, dst, phase, to):
        return pltpu.make_async_remote_copy(
            src_ref=src,
            dst_ref=dst,
            send_sem=send_sem.at[phase],
            recv_sem=recv_sem.at[phase],
            device_id=to,
            device_id_type=MESH,
        )

    def drain15(ref, sem):
        part = ref.at[pl.ds(0, 15)]
        pltpu.make_async_copy(part, part, sem).wait()

    b1[pl.ds(yx, 1)] = a0[pl.ds(yx, 1)]

    def scatter(k, _):
        t = (yx + k) % XY
        small(a0.at[t], b1.at[yx], 4, {"seq": z * XY + t}).start()
        return 0

    lax.fori_loop(1, XY, scatter, 0)

    drain15(b1, recv_sem.at[4])
    zc = z * 2 + core
    b2[pl.ds(zc, 1)] = jnp.sum(b1[...], axis=0, keepdims=True)

    def across(k, _):
        t = (zc + k) % XY
        small(b2.at[zc], b2.at[zc], 5, {"dp": t % 2, "seq": (t // 2) * XY + yx}).start()
        return 0

    lax.fori_loop(1, XY, across, 0)

    arrived(cs, cr, 2)
    gc[...] = nn(unmix, cr[...].reshape(R, HW)).astype(BF)

    @pl.loop(0, D // 256, unroll=True)
    def _(n):
        n0 = pl.multiple_of(n * 256, 256)
        part = nn(gc[...], wo[:, pl.ds(n0, 256)]).astype(BF).astype(F32)
        tokn = sums[3:4, pl.ds(n0, 256)]
        for s in range(2):
            xf = jnp.where(hcol[s] > 0.5, tokn, xv[s, :, pl.ds(n0, 256)].astype(F32))
            outv[s, :, pl.ds(n0, 256)] = (xf + part[s * L : (s + 1) * L]).astype(BF)

    out_copy = pltpu.make_async_copy(outv, out_hbm.at[0], out_sem.at[0])
    out_copy.start()
    drain15(b2, recv_sem.at[5])
    b3[pl.ds(yx, 1)] = jnp.sum(b2[...], axis=0, keepdims=True)

    def gather(k, _):
        t = (yx + k) % XY
        small(b3.at[yx], b3.at[yx], 6, {"seq": z * XY + t}).start()
        return 0

    lax.fori_loop(1, XY, gather, 0)

    def finish_step(i, _):
        dz = offset(i)
        f0 = pl.multiple_of(((z + NZ - dz) % NZ) * XY, XY)
        rows = []
        for half, dst in enumerate((nr, nr2)):
            block = dst.at[pl.ds(f0, XY)]
            pltpu.make_async_copy(block, block, plane_sem.at[half, dz]).wait()
            rows.append(dst[pl.ds(f0, XY)].reshape(2 * XY, HW))
        both = nn(unmix32, jnp.concatenate(rows, axis=1))
        for s in range(2):
            h = hcol[s, pl.ds(f0, XY), :] > 0.5
            rinv = rcol[s, pl.ds(f0, XY), :]
            xu = jnp.where(h, tok, xv[s, pl.ds(f0, XY), :].astype(F32)) * rinv
            g = both[s * XY : (s + 1) * XY] * gain
            mean = jnp.mean(g * xu, axis=1, keepdims=True)
            gi = cotv[s, pl.ds(f0, XY), :].astype(F32) + (g - xu * mean) * rinv
            gxv[s, pl.ds(f0, XY), :] = jnp.where(h, 0.0, gi).astype(BF)
        pltpu.make_async_copy(
            gxv.at[:, pl.ds(f0, XY)], gx_hbm.at[0, :, pl.ds(f0, XY)], out_sem.at[1]
        ).start()
        return 0

    lax.fori_loop(0, NZ, finish_step, 0)

    drain15(b3, recv_sem.at[6])
    for c in range(12):
        token_ref[:, c * 128 : (c + 1) * 128] = b3[c // 2, pl.ds(c % 2, 1), :]
        gain_out_ref[:, c * 128 : (c + 1) * 128] = b3[6 + c // 2, pl.ds(c % 2, 1), :]
    coef_out_ref[...] = b3[12, pl.ds(0, 1), :]

    drain(gs, send_sem.at[1])
    drain(cs, send_sem.at[2])
    drain(ns, send_sem.at[3])
    drain(ns2, send_sem.at[7])
    for phase, ref in ((4, a0), (5, b2), (6, b3)):
        drain15(ref, send_sem.at[phase])
    out_copy.wait()
    pltpu.make_async_copy(gxv, gx_hbm.at[0], out_sem.at[1]).wait()


def place_kernel(out_in, gx_in, token_in, gain_in, coef_in, out, gx, token, gain, coef, sem):
    copies = [
        pltpu.make_async_copy(out_in, out, sem.at[0]),
        pltpu.make_async_copy(gx_in, gx, sem.at[1]),
    ]
    for c in copies:
        c.start()
    token[...] = token_in[...].reshape(D)
    gain[...] = gain_in[...].reshape(D)
    coef[...] = coef_in[...].reshape(128)[:HEADS]
    for c in copies:
        c.wait()


def on_device(
    joints_x,
    cotangent,
    hidden,
    stream_clip,
    stream_kind,
    adjacency,
    mask_token,
    norm_gain,
    w_qkv,
    w_out,
    graph_coef,
):
    any_space = pl.BlockSpec(memory_space=pl.ANY)
    vmem = pl.BlockSpec(memory_space=pltpu.VMEM)
    smem = pl.BlockSpec(memory_space=pltpu.SMEM)
    dma = pltpu.SemaphoreType.DMA
    S = jax.ShapeDtypeStruct
    outs = pl.pallas_call(
        fused_kernel,
        out_shape=(
            S((1, 2, L, D), BF),
            S((1, 2, L, D), BF),
            S((1, D), F32),
            S((1, D), F32),
            S((1, 128), F32),
        ),
        in_specs=[any_space] * 10 + [smem],
        out_specs=(any_space, any_space, vmem, vmem, vmem),
        scratch_shapes=[
            pltpu.VMEM((2, L, D), BF),
            pltpu.VMEM((2, L, D), BF),
            pltpu.VMEM((1, 2, L), jnp.int32),
            pltpu.VMEM((1, R), jnp.int32),
            pltpu.VMEM((1, R), jnp.int32),
            pltpu.VMEM((KINDS, JM, JM), jnp.int32),
            pltpu.VMEM((D,), BF),
            pltpu.VMEM((D,), F32),
            pltpu.VMEM((D, 3 * HW), BF),
            pltpu.VMEM((HW, D), BF),
            pltpu.VMEM((2, L, D), BF),
            pltpu.VMEM((2, L, D), BF),
            pltpu.VMEM((NSEQ, 2, D), BF),
            pltpu.VMEM((NSEQ, 2, D), BF),
            pltpu.VMEM((NSEQ, 2, HW), BF),
            pltpu.VMEM((NSEQ, 2, HW), BF),
            pltpu.VMEM((NSEQ, 2, HW), BF),
            pltpu.VMEM((NSEQ, 2, HW), BF),
            pltpu.VMEM((NSEQ, 2, HW), BF),
            pltpu.VMEM((NSEQ, 2, HW), BF),
            pltpu.VMEM((NSEQ, 2, HW), BF),
            pltpu.VMEM((NSEQ, 2, HW), BF),
            pltpu.VMEM((2, L, 1), F32),
            pltpu.VMEM((2, L, 1), F32),
            pltpu.VMEM((R, 3 * HW), BF),
            pltpu.VMEM((R, D), BF),
            pltpu.VMEM((R, HW), BF),
            pltpu.VMEM((HW, R), BF),
            pltpu.VMEM((HW, R), BF),
            pltpu.VMEM((HW, R), BF),
            pltpu.VMEM((HW, R), BF),
            pltpu.VMEM((HEADS, R, R), BF),
            pltpu.VMEM((16, R), F32),
            pltpu.VMEM((R, 3 * HW), BF),
            pltpu.VMEM((R, R), F32),
            pltpu.VMEM((R, R), F32),
            pltpu.VMEM((16, R), F32),
            pltpu.VMEM((8, D), F32),
            pltpu.VMEM((R, D), BF),
            pltpu.VMEM((16, 2, 128), F32),
            pltpu.VMEM((16, 2, 128), F32),
            pltpu.VMEM((16, 2, 128), F32),
            pltpu.VMEM((16, 2, 128), F32),
            dma((10,)),
            dma((8,)),
            dma((7,)),
            dma((4,)),
            dma((2, NZ)),
            dma((2,)),
        ],
        compiler_params=pltpu.CompilerParams(
            collective_id=0, has_side_effects=True, vmem_limit_bytes=60 << 20
        ),
    )(
        joints_x,
        cotangent,
        hidden,
        stream_clip,
        stream_kind,
        adjacency,
        mask_token,
        norm_gain,
        w_qkv,
        w_out,
        graph_coef,
    )
    return pl.pallas_call(
        place_kernel,
        out_shape=(
            S((1, 2, L, D), BF),
            S((1, 2, L, D), BF),
            S((D,), F32),
            S((D,), F32),
            S((HEADS,), F32),
        ),
        in_specs=[vmem] * 5,
        out_specs=(any_space, any_space, vmem, vmem, vmem),
        scratch_shapes=[dma((2,))],
    )(*outs)


def solution(mesh):
    return jax.shard_map(
        on_device,
        mesh=mesh,
        in_specs=(
            P("dp", "seq", None, None),
            P("dp", "seq", None, None),
            P("dp", "seq", None),
            P("dp", None),
            P("dp", None),
            P(),
            P(),
            P(),
            P(),
            P(),
            P(),
        ),
        out_specs=(P("dp", "seq", None, None), P("dp", "seq", None, None), P(), P(), P()),
        check_vma=False,
    )
```

```python
import functools

import jax
import jax.numpy as jnp
from jax import lax
from jax.experimental import pallas as pl
from jax.experimental.pallas import tpu as pltpu
from jax.sharding import PartitionSpec as P

MESH = pl.DeviceIdType.MESH
BF = jnp.bfloat16
F32 = jnp.float32
NSEQ = 128
XY = 16
NZ = 8
D = 1536
HW = 768
HEADS = 12
HD = 64
R = 256
L = 128
KINDS = 4
JM = 136
PAIRS = HEADS // 2
MARK = 1000.0


def iota(shape, axis):
    return lax.broadcasted_iota(jnp.int32, shape, axis)


def nn(a, b):
    return jnp.dot(a, b, preferred_element_type=F32)


def nt(a, b):
    return lax.dot_general(a, b, (((1,), (1,)), ((), ())), preferred_element_type=F32)


def to_column(row, n):
    diag = iota((n, n), 0) == iota((n, n), 1)
    return jnp.sum(jnp.where(diag, row, jnp.zeros_like(row)), axis=1, keepdims=True)


def fused_kernel(
    x_hbm,
    cot_hbm,
    hid_hbm,
    clip_hbm,
    kind_hbm,
    adj_hbm,
    tok_hbm,
    gain_hbm,
    wqkv_hbm,
    wout_hbm,
    coef_ref,
    out_hbm,
    gx_hbm,
    token_ref,
    gain_out_ref,
    coef_out_ref,
    xv,
    cotv,
    hidv,
    clipv,
    kindv,
    adjv,
    tokv,
    gainv,
    wq,
    wo,
    outv,
    gxv,
    xs,
    xr,
    xs2,
    xr2,
    acc,
    gs,
    gr,
    cs,
    cr,
    ns,
    nr,
    ns2,
    nr2,
    hcol,
    rcol,
    qkv,
    xn,
    gc,
    vt,
    kt,
    ctt,
    dqt,
    pts,
    invs,
    du,
    link,
    bias,
    coefs,
    sums,
    tmp,
    a0,
    b1,
    b2,
    b3,
    in_sem,
    send_sem,
    recv_sem,
    loc_sem,
    plane_sem,
    out_sem,
):
    me = lax.axis_index("seq")
    core = lax.axis_index("dp")
    z = me // XY
    yx = me % XY
    y = yx // 4
    x = yx % 4

    loads = [
        (x_hbm.at[0], xv),
        (hid_hbm, hidv),
        (tok_hbm, tokv),
        (gain_hbm, gainv),
        (cot_hbm.at[0], cotv),
        (wout_hbm, wo),
        (clip_hbm, clipv),
        (kind_hbm, kindv),
        (adj_hbm, adjv),
        (wqkv_hbm, wq),
    ]
    load = [pltpu.make_async_copy(s, d, in_sem.at[i]) for i, (s, d) in enumerate(loads)]
    for c in load:
        c.start()

    barrier = pltpu.get_barrier_semaphore()

    def greet(k, _):
        pl.semaphore_signal(
            barrier, inc=1, device_id={"seq": (me + k) % NSEQ}, device_id_type=MESH
        )
        return 0

    lax.fori_loop(1, NSEQ, greet, 0)

    def greet_other(k, _):
        pl.semaphore_signal(
            barrier,
            inc=1,
            device_id={"dp": 1 - core, "seq": k * XY + yx},
            device_id_type=MESH,
        )
        return 0

    lax.fori_loop(0, NZ, greet_other, 0)

    for c in load[:4]:
        c.wait()
    tok = tokv[...].astype(F32).reshape(1, D)
    gain = gainv[...].reshape(1, D)
    sums[3:4, :] = tok
    hid = hidv[0].astype(F32)
    for s in range(2):
        hcol[s] = to_column(hid[s : s + 1, :], L)
    def peer(dz, dyx):
        return ((z + dz) % NZ) * XY + ((y + dyx // 4) % 4) * 4 + (x + dyx % 4) % 4

    def send(src, dst, phase, to):
        return pltpu.make_async_remote_copy(
            src_ref=src,
            dst_ref=dst,
            send_sem=send_sem.at[phase],
            recv_sem=recv_sem.at[phase],
            device_id={"seq": to},
            device_id_type=MESH,
        )

    def send_all(src, dst, phase):
        pltpu.make_async_copy(src.at[me], dst.at[me], loc_sem.at[phase]).start()

        def body(k, _):
            to = peer(k % NZ, k // NZ)
            send(src.at[to], dst.at[me], phase, to).start()
            return 0

        lax.fori_loop(1, NSEQ, body, 0)

    def drain(ref, sem):
        part = ref.at[pl.ds(0, NSEQ - 1)]
        pltpu.make_async_copy(part, part, sem).wait()

    def arrived(src, dst, phase):
        pltpu.make_async_copy(src.at[me], dst.at[me], loc_sem.at[phase]).wait()
        drain(dst, recv_sem.at[phase])

    r32, c32 = iota((32, 32), 0), iota((32, 32), 1)
    mix32 = (c32 == (r32 % 2) * 16 + r32 // 2).astype(BF)

    def offset(i):
        near = i // 2 + 1
        return jnp.where(i == NZ - 1, 0, jnp.where(i % 2 == 1, NZ - near, near))

    def norm_step(i, _):
        zz = (z + offset(i)) % NZ
        f0 = pl.multiple_of(zz * XY, XY)
        parts = []
        for s in range(2):
            xf = xv[s, pl.ds(f0, XY), :].astype(F32)
            h = hcol[s, pl.ds(f0, XY), :]
            xf = jnp.where(h > 0.5, tok, xf)
            rinv = 1.0 / jnp.sqrt(jnp.mean(xf * xf, axis=1, keepdims=True) + 1e-06)
            rcol[s, pl.ds(f0, XY), :] = rinv
            row = xf * rinv * gain
            mark = (h > 0.5) & (iota((XY, D), 1) == 0)
            parts.append(jnp.where(mark, MARK, row).astype(BF))
        both = nn(mix32, jnp.concatenate(parts, axis=0)).astype(BF)
        xs[pl.ds(f0, XY)] = both[:, :HW].reshape(XY, 2, HW)
        xs2[pl.ds(f0, XY)] = both[:, HW:].reshape(XY, 2, HW)

        @pl.when(i == 0)
        def _():
            pl.semaphore_wait(barrier, NSEQ - 1 + NZ)

        def body(k, _):
            to = zz * XY + ((y + k // 4) % 4) * 4 + (x + k % 4) % 4

            @pl.when(to != me)
            def _():
                send(xs.at[to], xr.at[me], 0, to).start()

            return 0

        lax.fori_loop(0, XY, body, 0)
        return 0

    lax.fori_loop(0, NZ, norm_step, 0)
    pltpu.make_async_copy(xs.at[me], xr.at[me], loc_sem.at[0]).start()
    send_all(xs2, xr2, 3)

    ri, ci = iota((R, R), 0), iota((R, R), 1)
    mix = (ci == (ri % 2) * L + ri // 2).astype(BF)
    unmix = (ci == (ri % L) * 2 + ri // L).astype(BF)
    unmix32 = (c32 == (r32 % XY) * 2 + r32 // XY).astype(BF)
    for c in load[4:6]:
        c.wait()

    @pl.loop(0, HW // 256, unroll=True)
    def _(n):
        n0 = pl.multiple_of(n * 256, 256)
        part = nt(cotv[...].reshape(R, D), wo[pl.ds(n0, 256), :]).astype(BF)
        tmp[:, pl.ds(n0, 256)] = nn(mix, part).astype(BF)

    gs[...] = tmp[:, :HW].reshape(NSEQ, 2, HW)
    scot = jnp.zeros((8, D), F32)
    for s in range(2):
        picks = jnp.broadcast_to(hid[s : s + 1, :], (8, L)).astype(BF)
        scot = scot + nn(picks, cotv[s])
    sums[0:1, :] = scot[0:1]
    send_all(gs, gr, 1)

    for c in load[6:9]:
        c.wait()
    clip_row = clipv[...]
    clip_col = to_column(clip_row, R)
    same = clip_col == clip_row
    first_row = jnp.min(jnp.where(same, ri, R), axis=0, keepdims=True)
    first_col = to_column(first_row, R)
    kind_col = to_column(kindv[...], R)
    joint_col = iota((R, 1), 0) - first_col
    pick = iota((R, JM), 1) == joint_col
    picked = jnp.zeros((R, JM), F32)
    for k in range(KINDS):
        rows = (pick & (kind_col == k)).astype(BF)
        picked = picked + nn(rows, adjv[k].astype(F32).astype(BF))
    link[...] = nt(pick.astype(BF), picked.astype(BF))
    bias[...] = jnp.where(same, link[...], -jnp.inf)

    load[9].wait()
    arrived(xs, xr, 0)
    xn[:, :HW] = xr[...].reshape(R, HW)
    head = xn[:, :128]
    flag_col = jnp.where(head[:, 0:1].astype(F32) > MARK / 2, 1.0, 0.0)
    flag_row = jnp.sum(jnp.where(ri == ci, flag_col, 0.0), axis=0, keepdims=True)
    flags = jnp.broadcast_to(flag_row, (8, R)).astype(BF)
    tok_rinv = 1.0 / jnp.sqrt(jnp.mean(tok * tok, axis=1, keepdims=True) + 1e-06)
    tok_unit = tok * tok_rinv
    tok_head = (tok_unit * gain)[:, :128].astype(BF).astype(F32)
    fix = (flag_col > 0.5) & (iota((R, 128), 1) == 0)
    xn[:, :128] = jnp.where(fix, tok_head, head.astype(F32)).astype(BF)

    @pl.loop(0, 3 * HW // 256, unroll=True)
    def _(n):
        n0 = pl.multiple_of(n * 256, 256)
        acc[:, pl.ds(n0, 256)] = nn(xn[:, :HW], wq[:HW, pl.ds(n0, 256)])

    arrived(xs2, xr2, 3)
    xn[:, HW:] = xr2[...].reshape(R, HW)

    @pl.loop(0, 3 * HW // 256, unroll=True)
    def _(n):
        n0 = pl.multiple_of(n * 256, 256)
        part = acc[:, pl.ds(n0, 256)] + nn(xn[:, HW:], wq[HW:, pl.ds(n0, 256)])
        part = part.astype(BF)
        scale = jnp.where(n < HW // 256, HD**-0.5, 1.0).astype(BF)
        qkv[:, pl.ds(n0, 256)] = part * scale

    coefs[...] = jnp.zeros_like(coefs)
    kt[...] = qkv[:, HW : 2 * HW].T
    vt[...] = qkv[:, 2 * HW :].T

    lane = iota((R, 128), 1)

    @pl.loop(0, PAIRS, unroll=True)
    def _(j):
        c0 = pl.multiple_of(j * 128, 128)
        q2 = qkv[:, pl.ds(c0, 128)]
        k2 = qkv[:, pl.ds(HW + c0, 128)]
        for i in range(2):
            h = j * 2 + i
            r0 = pl.multiple_of(h * HD, HD)
            kh = jnp.where((lane < HD) == (i == 0), k2, jnp.zeros_like(k2))
            rows = []
            for half in range(2):
                cols = slice(half * 128, half * 128 + 128)
                st = nt(kh, q2[cols]) + coef_ref[h] * bias[:, cols]
                e = jnp.exp(st - jnp.max(st, axis=0, keepdims=True))
                inv = 1.0 / jnp.sum(e, axis=0, keepdims=True)
                eb = e.astype(BF)
                pts[h, :, cols] = e
                rows.append(inv)
                ct = nn(vt[pl.ds(r0, HD), :], eb) * inv
                ctt[pl.ds(r0, HD), cols] = ct.astype(BF)
            invs[pl.ds(h, 1), :] = jnp.concatenate(rows, axis=1)

    cs[...] = ctt[...].T.reshape(NSEQ, 2, HW)
    send_all(cs, cr, 2)

    arrived(gs, gr, 1)
    gc[...] = gr[...].reshape(R, HW)

    @pl.loop(0, PAIRS, unroll=True)
    def _(j):
        c0 = pl.multiple_of(j * 128, 128)
        q2 = qkv[:, pl.ds(c0, 128)]
        v2 = qkv[:, pl.ds(2 * HW + c0, 128)]
        g2 = gc[:, pl.ds(c0, 128)]
        dk, dv = [], []
        for i in range(2):
            h = j * 2 + i
            r0 = pl.multiple_of(h * HD, HD)
            vh = jnp.where((lane < HD) == (i == 0), v2, jnp.zeros_like(v2))
            dbs, pbs, rows = [], [], []
            inv = invs[pl.ds(h, 1), :]
            for half in range(2):
                cols = slice(half * 128, half * 128 + 128)
                p = pts[h, :, cols] * inv[:, cols]
                dp = nt(vh, g2[cols])
                ds = p * (dp - jnp.sum(p * dp, axis=0, keepdims=True))
                rows.append(jnp.sum(ds * link[:, cols], axis=0, keepdims=True))
                db = ds.astype(BF)
                dq = nn(kt[pl.ds(r0, HD), :], db) * (HD**-0.5)
                dqt[pl.ds(r0, HD), cols] = dq.astype(BF)
                dbs.append(db)
                pbs.append(p.astype(BF))
            coefs[pl.ds(h, 1), :] = jnp.concatenate(rows, axis=1)
            dk.append(nn(jnp.concatenate(dbs, axis=1), q2))
            dv.append(nn(jnp.concatenate(pbs, axis=1), g2))
        du[:, pl.ds(HW + c0, 128)] = jnp.where(lane < HD, dk[0], dk[1]).astype(BF)
        du[:, pl.ds(2 * HW + c0, 128)] = jnp.where(lane < HD, dv[0], dv[1]).astype(BF)

    du[:, :HW] = dqt[...].T

    for half, (src, dst) in enumerate(((ns, nr), (ns2, nr2))):

        @pl.loop(0, HW // 256, unroll=True)
        def _(n, half=half):
            n0 = pl.multiple_of(half * HW + n * 256, 256)
            gn = nt(du[...], wq[pl.ds(n0, 256), :]).astype(BF)
            tmp[:, pl.ds(n0, 256)] = gn
            sums[1:2, pl.ds(n0, 256)] = nn(flags, gn)[0:1]
            prod = gn.astype(F32) * xn[:, pl.ds(n0, 256)].astype(F32)
            sums[2:3, pl.ds(n0, 256)] = jnp.sum(prod, axis=0, keepdims=True)

        src[...] = tmp[:, half * HW : half * HW + HW].reshape(NSEQ, 2, HW)

        def send_plane(i, _, src=src, dst=dst, half=half):
            dz = offset(i)

            def body(k, _):
                to = peer(dz, k)

                @pl.when(to != me)
                def _():
                    pltpu.make_async_remote_copy(
                        src_ref=src.at[to],
                        dst_ref=dst.at[me],
                        send_sem=send_sem.at[8 - half],
                        recv_sem=plane_sem.at[half, dz],
                        device_id={"seq": to},
                        device_id_type=MESH,
                    ).start()

                return 0

            lax.fori_loop(0, XY, body, 0)
            return 0

        lax.fori_loop(0, NZ, send_plane, 0)
        pltpu.make_async_copy(src.at[me], dst.at[me], plane_sem.at[half, 0]).start()

    sgn = gain * sums[1:2, :]
    token_sum = sgn - tok_unit * jnp.mean(sgn * tok_unit, axis=1, keepdims=True)
    token_sum = sums[0:1, :] + token_sum * tok_rinv
    gain_sum = sums[2:3, :] / gain
    coef_col = jnp.sum(coefs[...], axis=1, keepdims=True)
    coef_row = jnp.sum(
        jnp.where(iota((16, 128), 0) == iota((16, 128), 1), coef_col, 0.0), axis=0, keepdims=True
    )
    a0[...] = jnp.zeros_like(a0)
    for c in range(12):
        a0[c // 2, pl.ds(c % 2, 1), :] = token_sum[:, c * 128 : (c + 1) * 128]
        a0[6 + c // 2, pl.ds(c % 2, 1), :] = gain_sum[:, c * 128 : (c + 1) * 128]
    a0[12, pl.ds(0, 1), :] = coef_row

    def small(src, dst, phase, to):
        return pltpu.make_async_remote_copy(
            src_ref=src,
            dst_ref=dst,
            send_sem=send_sem.at[phase],
            recv_sem=recv_sem.at[phase],
            device_id=to,
            device_id_type=MESH,
        )

    def drain15(ref, sem):
        part = ref.at[pl.ds(0, 15)]
        pltpu.make_async_copy(part, part, sem).wait()

    b1[pl.ds(yx, 1)] = a0[pl.ds(yx, 1)]

    def scatter(k, _):
        t = (yx + k) % XY
        small(a0.at[t], b1.at[yx], 4, {"seq": z * XY + t}).start()
        return 0

    lax.fori_loop(1, XY, scatter, 0)

    drain15(b1, recv_sem.at[4])
    zc = z * 2 + core
    b2[pl.ds(zc, 1)] = jnp.sum(b1[...], axis=0, keepdims=True)

    def across(k, _):
        t = (zc + k) % XY
        small(b2.at[zc], b2.at[zc], 5, {"dp": t % 2, "seq": (t // 2) * XY + yx}).start()
        return 0

    lax.fori_loop(1, XY, across, 0)

    arrived(cs, cr, 2)
    gc[...] = nn(unmix, cr[...].reshape(R, HW)).astype(BF)

    @pl.loop(0, D // 256, unroll=True)
    def _(n):
        n0 = pl.multiple_of(n * 256, 256)
        part = nn(gc[...], wo[:, pl.ds(n0, 256)]).astype(BF).astype(F32)
        tokn = sums[3:4, pl.ds(n0, 256)]
        for s in range(2):
            xf = jnp.where(hcol[s] > 0.5, tokn, xv[s, :, pl.ds(n0, 256)].astype(F32))
            outv[s, :, pl.ds(n0, 256)] = (xf + part[s * L : (s + 1) * L]).astype(BF)

    out_copy = pltpu.make_async_copy(outv, out_hbm.at[0], out_sem.at[0])
    out_copy.start()
    drain15(b2, recv_sem.at[5])
    b3[pl.ds(yx, 1)] = jnp.sum(b2[...], axis=0, keepdims=True)

    def gather(k, _):
        t = (yx + k) % XY
        small(b3.at[yx], b3.at[yx], 6, {"seq": z * XY + t}).start()
        return 0

    lax.fori_loop(1, XY, gather, 0)

    def finish_step(i, _):
        dz = offset(i)
        f0 = pl.multiple_of(((z + NZ - dz) % NZ) * XY, XY)
        rows = []
        for half, dst in enumerate((nr, nr2)):
            block = dst.at[pl.ds(f0, XY)]
            pltpu.make_async_copy(block, block, plane_sem.at[half, dz]).wait()
            rows.append(dst[pl.ds(f0, XY)].reshape(2 * XY, HW))
        both = nn(unmix32, jnp.concatenate(rows, axis=1))
        for s in range(2):
            h = hcol[s, pl.ds(f0, XY), :] > 0.5
            rinv = rcol[s, pl.ds(f0, XY), :]
            xu = jnp.where(h, tok, xv[s, pl.ds(f0, XY), :].astype(F32)) * rinv
            g = both[s * XY : (s + 1) * XY] * gain
            mean = jnp.mean(g * xu, axis=1, keepdims=True)
            gi = cotv[s, pl.ds(f0, XY), :].astype(F32) + (g - xu * mean) * rinv
            gxv[s, pl.ds(f0, XY), :] = jnp.where(h, 0.0, gi).astype(BF)
        pltpu.make_async_copy(
            gxv.at[:, pl.ds(f0, XY)], gx_hbm.at[0, :, pl.ds(f0, XY)], out_sem.at[1]
        ).start()
        return 0

    lax.fori_loop(0, NZ, finish_step, 0)

    drain15(b3, recv_sem.at[6])
    for c in range(12):
        token_ref[:, c * 128 : (c + 1) * 128] = b3[c // 2, pl.ds(c % 2, 1), :]
        gain_out_ref[:, c * 128 : (c + 1) * 128] = b3[6 + c // 2, pl.ds(c % 2, 1), :]
    coef_out_ref[...] = b3[12, pl.ds(0, 1), :]

    drain(xs, send_sem.at[0])
    drain(gs, send_sem.at[1])
    drain(cs, send_sem.at[2])
    drain(xs2, send_sem.at[3])
    drain(ns, send_sem.at[8])
    drain(ns2, send_sem.at[7])
    for phase, ref in ((4, a0), (5, b2), (6, b3)):
        drain15(ref, send_sem.at[phase])
    out_copy.wait()
    pltpu.make_async_copy(gxv, gx_hbm.at[0], out_sem.at[1]).wait()


def place_kernel(out_in, gx_in, token_in, gain_in, coef_in, out, gx, token, gain, coef, sem):
    copies = [
        pltpu.make_async_copy(out_in, out, sem.at[0]),
        pltpu.make_async_copy(gx_in, gx, sem.at[1]),
    ]
    for c in copies:
        c.start()
    token[...] = token_in[...].reshape(D)
    gain[...] = gain_in[...].reshape(D)
    coef[...] = coef_in[...].reshape(128)[:HEADS]
    for c in copies:
        c.wait()


def on_device(
    joints_x,
    cotangent,
    hidden,
    stream_clip,
    stream_kind,
    adjacency,
    mask_token,
    norm_gain,
    w_qkv,
    w_out,
    graph_coef,
):
    any_space = pl.BlockSpec(memory_space=pl.ANY)
    vmem = pl.BlockSpec(memory_space=pltpu.VMEM)
    smem = pl.BlockSpec(memory_space=pltpu.SMEM)
    dma = pltpu.SemaphoreType.DMA
    S = jax.ShapeDtypeStruct
    outs = pl.pallas_call(
        fused_kernel,
        out_shape=(
            S((1, 2, L, D), BF),
            S((1, 2, L, D), BF),
            S((1, D), F32),
            S((1, D), F32),
            S((1, 128), F32),
        ),
        in_specs=[any_space] * 10 + [smem],
        out_specs=(any_space, any_space, vmem, vmem, vmem),
        scratch_shapes=[
            pltpu.VMEM((2, L, D), BF),
            pltpu.VMEM((2, L, D), BF),
            pltpu.VMEM((1, 2, L), jnp.int32),
            pltpu.VMEM((1, R), jnp.int32),
            pltpu.VMEM((1, R), jnp.int32),
            pltpu.VMEM((KINDS, JM, JM), jnp.int32),
            pltpu.VMEM((D,), BF),
            pltpu.VMEM((D,), F32),
            pltpu.VMEM((D, 3 * HW), BF),
            pltpu.VMEM((HW, D), BF),
            pltpu.VMEM((2, L, D), BF),
            pltpu.VMEM((2, L, D), BF),
            pltpu.VMEM((NSEQ, 2, HW), BF),
            pltpu.VMEM((NSEQ, 2, HW), BF),
            pltpu.VMEM((NSEQ, 2, HW), BF),
            pltpu.VMEM((NSEQ, 2, HW), BF),
            pltpu.VMEM((R, 3 * HW), F32),
            pltpu.VMEM((NSEQ, 2, HW), BF),
            pltpu.VMEM((NSEQ, 2, HW), BF),
            pltpu.VMEM((NSEQ, 2, HW), BF),
            pltpu.VMEM((NSEQ, 2, HW), BF),
            pltpu.VMEM((NSEQ, 2, HW), BF),
            pltpu.VMEM((NSEQ, 2, HW), BF),
            pltpu.VMEM((NSEQ, 2, HW), BF),
            pltpu.VMEM((NSEQ, 2, HW), BF),
            pltpu.VMEM((2, L, 1), F32),
            pltpu.VMEM((2, L, 1), F32),
            pltpu.VMEM((R, 3 * HW), BF),
            pltpu.VMEM((R, D), BF),
            pltpu.VMEM((R, HW), BF),
            pltpu.VMEM((HW, R), BF),
            pltpu.VMEM((HW, R), BF),
            pltpu.VMEM((HW, R), BF),
            pltpu.VMEM((HW, R), BF),
            pltpu.VMEM((HEADS, R, R), F32),
            pltpu.VMEM((16, R), F32),
            pltpu.VMEM((R, 3 * HW), BF),
            pltpu.VMEM((R, R), F32),
            pltpu.VMEM((R, R), F32),
            pltpu.VMEM((16, R), F32),
            pltpu.VMEM((8, D), F32),
            pltpu.VMEM((R, D), BF),
            pltpu.VMEM((16, 2, 128), F32),
            pltpu.VMEM((16, 2, 128), F32),
            pltpu.VMEM((16, 2, 128), F32),
            pltpu.VMEM((16, 2, 128), F32),
            dma((10,)),
            dma((9,)),
            dma((7,)),
            dma((4,)),
            dma((2, NZ)),
            dma((2,)),
        ],
        compiler_params=pltpu.CompilerParams(
            collective_id=0, has_side_effects=True, vmem_limit_bytes=60 << 20
        ),
    )(
        joints_x,
        cotangent,
        hidden,
        stream_clip,
        stream_kind,
        adjacency,
        mask_token,
        norm_gain,
        w_qkv,
        w_out,
        graph_coef,
    )
    return pl.pallas_call(
        place_kernel,
        out_shape=(
            S((1, 2, L, D), BF),
            S((1, 2, L, D), BF),
            S((D,), F32),
            S((D,), F32),
            S((HEADS,), F32),
        ),
        in_specs=[vmem] * 5,
        out_specs=(any_space, any_space, vmem, vmem, vmem),
        scratch_shapes=[dma((2,))],
    )(*outs)


def solution(mesh):
    return jax.shard_map(
        on_device,
        mesh=mesh,
        in_specs=(
            P("dp", "seq", None, None),
            P("dp", "seq", None, None),
            P("dp", "seq", None),
            P("dp", None),
            P("dp", None),
            P(),
            P(),
            P(),
            P(),
            P(),
            P(),
        ),
        out_specs=(P("dp", "seq", None, None), P("dp", "seq", None, None), P(), P(), P()),
        check_vma=False,
    )
```
